256 devices in a mesh: mesh: 2 (over y_lo), seq: 8 (over x, core), fsdp: 16 (over z, y_hi).
Axes of the slice: x: 4, y: 4 (y_hi: 2, y_lo: 2; y = y_hi * 2 + y_lo), z: 8, core: 2. Of those that a mesh axis runs over, the one named last changes fastest.
Arguments:
- latents: bfloat16 [16, 512, 5120], P('fsdp', 'mesh'), may hold values from -8 to 8
- noise: bfloat16 [16, 512, 5120], P('fsdp', 'mesh'), may hold values from -6 to 6
- noise_level: float32 [16], P('fsdp'), may hold values from 0.05 to 0.3
- group_index: int32 [16, 512], P('fsdp'), may hold values from 0 to 7, never falling along the last dimension, each value on 1 to 128 neighbouring positions
- projections: bfloat16 [2, 5120, 3, 3072], P('mesh', 'fsdp', None, 'seq'), may hold values from -1 to 1, as said below
- upstream: bfloat16 [16, 512, 3072], P('fsdp', None, 'seq'), may hold values from -0.29882812 to 0.29882812
Outputs:
- direction: bfloat16 [16, 512, 3072], P('fsdp', ('mesh', 'seq'))
- fake_grads: float32 [5120, 3, 3072], P(('mesh', 'fsdp'), None, 'seq')
The draws below stay inside these ranges and needn't reach their ends.
Inputs may be any that keep to these rules, and one draw needn't show every extreme that they name: `projections`: along the third dimension: query, key and value projection, in that order. `group_index`: along each clip the group numbers never fall; each of the 8 groups holds 1 to 128 tokens.
All inputs are finite; a program needn't handle non-finite values.
Results may differ from the reference program's by a relative error of at most 0.018.
Values may be sent and summed in bfloat16 or wider, within the bound.
A program may use at most 128 MiB of HBM per device.

```python
import math
import jax
import jax.numpy as jnp
import numpy as np
from jax import lax

D = 5120
HEAD = 128
HEADS = 24
LEN = 512
GROUPS = 8
GROUP_MOST = 128
CLIPS = 16


def draw_latents(key, part):
    normal_rows = jax.random.normal(jax.random.fold_in(key, 11), (CLIPS, LEN, D), jnp.float32)
    drawn = jnp.clip(normal_rows, -6.0, 6.0)
    return drawn.astype(jnp.bfloat16)


def draw_projections(key, part):
    normal_rows = jax.random.normal(jax.random.fold_in(key, 21), (2, D, 3, HEADS * HEAD), jnp.float32) / math.sqrt(D)
    drawn = normal_rows
    return drawn.astype(jnp.bfloat16)


def steps_of(own_key, extent, split, least, top_value):
    factor_of = 1.0
    for axis_at, shards_of in split:
        steps = jax.random.uniform(jax.random.fold_in(jax.random.fold_in(own_key, 6), axis_at), (shards_of,), jnp.float32, least / len(split), top_value / len(split))
        factor_of = factor_of * jnp.repeat(jnp.exp(steps), extent[axis_at] // shards_of).reshape((-1,) + (1,) * (len(extent) - 1 - axis_at))
    return factor_of


def split_up(amount, total, reach, lean):
    weights = [(1 << 20) // math.isqrt(rank ** lean) + 1 for rank in range(2, amount + 1)]
    rest, counts = total - reach - (amount - 1), [1] * (amount - 1)
    while rest > 0:
        movable = [i for i in range(amount - 1) if counts[i] < reach]
        mass, budget = sum([weights[i] for i in movable]), rest
        for i in movable:
            addition = min(reach - counts[i], max(1, budget * weights[i] // mass), rest)
            counts[i] = counts[i] + addition
            rest = rest - addition
    return np.array([reach] + counts)


def uneven(rng, number_of, total, most, lean):
    if number_of == 2:
        one = jax.random.randint(rng, (), max(1, total - most), min(most, total - 1) + 1)
        return jnp.stack([one, total - one])
    lengths = jnp.asarray(split_up(number_of, total, most, lean), jnp.int32)
    twos = (number_of - 1) // 2
    giver, taker = lengths[1:1 + 2 * twos:2], lengths[2:2 + 2 * twos:2]
    margin = jnp.minimum(giver - 1, most - taker)
    moved = jax.random.randint(jax.random.fold_in(rng, 1), (twos,), 0, 1 << 20) % (margin + 1)
    lengths = lengths.at[1:1 + 2 * twos:2].set(giver - moved).at[2:2 + 2 * twos:2].set(taker + moved)
    return lengths[jax.random.permutation(jax.random.fold_in(rng, 2), number_of)]


def centred(key, extent, deviation, most, pieces=(), held_as=jnp.bfloat16):
    loudness = steps_of(key, extent, pieces, -0.22, 0.18) if pieces else 1.0
    result = jax.random.normal(key, extent, jnp.float32) * deviation * loudness
    return jnp.minimum(jnp.maximum(result, -most), most).astype(held_as)


def setup_inputs(seed: int = 0) -> dict:
    key_of = jax.random.split(jax.random.key(seed), 7)
    latents = draw_latents(jax.random.fold_in(key_of[6], 71), 0)
    noise = centred(key_of[1], (CLIPS, LEN, D), 1.0, 6.0, ((0, 16), (1, 2)))
    noise_level = jnp.clip(jnp.exp(math.log(0.3) - 1.7917595 * jax.random.uniform(key_of[2], (CLIPS,), jnp.float32) ** steps_of(key_of[2], (CLIPS,), ((0, 16),), -0.2, 0.2)), 0.05, 0.3)
    group_index = jax.vmap(lambda own: jnp.searchsorted(jnp.cumsum(uneven(own, GROUPS, LEN, GROUP_MOST, 1)), jnp.arange(LEN), side="right"))(jax.random.split(key_of[3], CLIPS)).reshape((CLIPS, LEN)).astype(jnp.int32)
    projections = draw_projections(jax.random.fold_in(key_of[6], 71), 0)
    upstream = centred(key_of[5], (CLIPS, LEN, HEADS * HEAD), 0.05, 0.29882812, ((0, 16), (2, 8)))
    return {"latents": latents, "noise": noise, "noise_level": noise_level, "group_index": group_index, "projections": projections, "upstream": upstream}


def attend(queries, key_rows, values, visible, score_scale):
    scores = jnp.einsum('qhd,khd->hqk', queries.astype(jnp.float32), key_rows.astype(jnp.float32)) * score_scale
    scores = jnp.where(visible[None], scores, jnp.float32(-1e+30))
    highest = lax.optimization_barrier(jnp.max(scores, axis=-1, keepdims=True))
    weights = jnp.exp(scores - highest)
    probabilities = weights / lax.optimization_barrier(jnp.sum(weights, axis=-1, keepdims=True))
    prob_low = probabilities.astype(jnp.bfloat16)
    attended = jnp.einsum('hqk,khd->qhd', prob_low.astype(jnp.float32), values.astype(jnp.float32)).astype(jnp.bfloat16)
    return (probabilities, prob_low, attended)

def reference(latents, noise, noise_level, group_index, projections, upstream):
    head_cols = HEADS * HEAD
    score_scale = 1.0 / math.sqrt(HEAD)

    def one_clip(running, inputs):
        clip_rows, clip_noise, noise_rate, groups, clip_upstream = inputs
        noised = ((1.0 - noise_rate) * clip_rows.astype(jnp.float32) + noise_rate * clip_noise.astype(jnp.float32)).astype(jnp.bfloat16)
        visible = groups[None, :] <= groups[:, None]
        outputs = []
        for model in range(2):
            triple = jnp.dot(noised, projections[model].reshape(D, 3 * head_cols), preferred_element_type=jnp.float32)
            triple = triple.astype(jnp.bfloat16).reshape(LEN, 3, HEADS, HEAD)
            outputs.append((triple, attend(triple[:, 0], triple[:, 1], triple[:, 2], visible, score_scale)))
        teacher_out = outputs[0][1][2].reshape(LEN, head_cols)
        fake_triple, fake_parts = outputs[1]
        probabilities, prob_low, fake_out = fake_parts
        direction = (fake_out.reshape(LEN, head_cols).astype(jnp.float32) - teacher_out.astype(jnp.float32)).astype(jnp.bfloat16)
        grad_out = clip_upstream.reshape(LEN, HEADS, HEAD).astype(jnp.float32)
        queries = fake_triple[:, 0].astype(jnp.float32)
        key_rows = fake_triple[:, 1].astype(jnp.float32)
        values = fake_triple[:, 2].astype(jnp.float32)
        value_grad = jnp.einsum('hqk,qhd->khd', prob_low.astype(jnp.float32), grad_out).astype(jnp.bfloat16)
        prob_grad = jnp.einsum('qhd,khd->hqk', grad_out, values)
        row_inner = lax.optimization_barrier(jnp.sum(probabilities * prob_grad, axis=-1, keepdims=True))
        score_grad = (probabilities * (prob_grad - row_inner) * score_scale).astype(jnp.bfloat16)
        query_grad = jnp.einsum('hqk,khd->qhd', score_grad.astype(jnp.float32), key_rows).astype(jnp.bfloat16)
        key_grad = jnp.einsum('hqk,qhd->khd', score_grad.astype(jnp.float32), queries).astype(jnp.bfloat16)
        cotangents = jnp.stack([query_grad, key_grad, value_grad], axis=1).reshape(LEN, 3 * head_cols)
        partial_value = lax.dot_general(noised, cotangents, (((0,), (0,)), ((), ())), preferred_element_type=jnp.float32)
        return (running + partial_value.astype(jnp.bfloat16).astype(jnp.float32), direction)
    zero_sum = jnp.zeros((D, 3 * head_cols), jnp.float32)
    summed, direction = lax.scan(one_clip, zero_sum, (latents, noise, noise_level, group_index, upstream))
    return (direction, summed.reshape(D, 3, head_cols))
```

```python
import math

import jax
import jax.numpy as jnp
from jax import lax
from jax.experimental import pallas as pl
from jax.experimental.pallas import tpu as pltpu
from jax.sharding import Mesh
from jax.sharding import PartitionSpec as P

HEAD = 128
AXES = ("m", "x", "c", "z", "yh")
MESH_ID = pl.DeviceIdType.MESH
F32 = jnp.float32
BF16 = jnp.bfloat16
OFFSETS = (0, -1, 1, -2, 2, -3, 3, 4)
GROUP_ORDER = (1, 2, 0)


def dot(a, b, dims):
    return lax.dot_general(a, b, (dims, ((), ())), preferred_element_type=F32)


def step_kernel(
    lat_ref, noi_ref, lvl_ref, proj_ref, up_ref, gi_ref,
    dir_ref, grad_ref,
    wbuf, xbuf, latv, noiv, acc, tri, upb, gib, gcol, attb, cotb, coto,
    xts, xto, pbuf, dsbuf, gbuf, sbuf, rbuf, fbuf, obuf, dbuf,
    wr, wc, ws, wcs, wos, xr, xs, lsem, usem, xtr, xtss, cr, cs, er, es,
    rr, rs, fr, fs, dr, dsm,
):
    m, x, c, z, yh = (lax.axis_index(a) for a in AXES)
    nz = lax.axis_size("z")
    nx = lax.axis_size("x")
    home = c == yh
    away = c != yh

    def at(**k):
        return k

    core_p = at(c=1 - c)
    sib = at(m=1 - m)
    out = at(m=1 - m, yh=1 - yh)
    turn = at(c=yh, yh=c)
    up_z = at(z=lax.rem(z + 1, nz))
    dn_z = at(z=lax.rem(z + nz - 1, nz))
    blk = [lax.rem(z + nz + o, nz) for o in OFFSETS]

    def rcopy(src, dst, ss, rsem, dev):
        return pltpu.make_async_remote_copy(
            src_ref=src, dst_ref=dst, send_sem=ss, recv_sem=rsem,
            device_id=dev, device_id_type=MESH_ID,
        )

    def wait_on(ref, sem):
        pltpu.make_async_copy(ref, ref, sem).wait()

    pending = []

    def send(cp, cond=None):
        if cond is None:
            cp.start()
        else:
            pl.when(cond)(cp.start)
        pending.append((cp, cond))

    rows_m = pl.ds(pl.multiple_of(m * 256, 256), 256)
    rows_o = pl.ds(pl.multiple_of((1 - m) * 256, 256), 256)

    def lane(k):
        return pl.ds(pl.multiple_of(blk[k] * 640, 128), 640)

    def read(k, which):
        src, dst = ((lat_ref, latv), (noi_ref, noiv))[which]
        return pltpu.make_async_copy(src.at[:, lane(k)], dst.at[k], lsem.at[k, which])

    w_half = [pl.ds(pl.multiple_of(c * 320 + 160 * i, 16), 160) for i in range(2)]
    w_home = [pl.ds(pl.multiple_of(yh * 320 + 160 * i, 16), 160) for i in range(2)]

    @pl.when(home)
    def _():
        for i in range(2):
            for j in range(3):
                pltpu.make_async_copy(
                    proj_ref.at[j, pl.ds(160 * i, 160), :],
                    wbuf.at[z, w_home[i], pl.ds(384 * j, 384)], wr.at[0, i],
                ).start()
        for k in range(8):
            read(k, 0).start()
            read(k, 1).start()

    barrier = pltpu.get_barrier_semaphore()
    count = 0
    for dm in range(2):
        for dx in range(4):
            for dc in range(2):
                for dy in range(2):
                    if dm + dx + dc + dy == 0:
                        continue
                    peer = at(
                        m=lax.rem(m + dm, 2), x=lax.rem(x + dx, nx),
                        c=lax.rem(c + dc, 2), yh=lax.rem(yh + dy, 2),
                    )
                    pl.semaphore_signal(barrier, inc=1, device_id=peer, device_id_type=MESH_ID)
                    count += 1
    for peer in (up_z, dn_z):
        pl.semaphore_signal(barrier, inc=1, device_id=peer, device_id_type=MESH_ID)
        count += 1
    pl.semaphore_wait(barrier, count)

    for i in range(2):
        for j in range(3):
            send(
                rcopy(
                    proj_ref.at[j, pl.ds(160 * i, 160), :],
                    wbuf.at[z, w_home[i], pl.ds(384 * j, 384)],
                    wos.at[i, j], wr.at[0, i], turn,
                ),
                away,
            )
    send(rcopy(gi_ref, gib, usem.at[2], usem.at[3], turn), away)
    up_keep = jnp.logical_or(home, m == 0)
    up_move = jnp.logical_and(away, m == 1)
    send(rcopy(up_ref, upb, usem.at[0], usem.at[1], turn), up_move)

    @pl.when(up_keep)
    def _():
        pltpu.make_async_copy(up_ref, upb, usem.at[1]).start()

    @pl.when(home)
    def _():
        pltpu.make_async_copy(gi_ref, gib, usem.at[3]).start()

    rate = lvl_ref[0]

    def noise(k):
        @pl.when(home)
        def _():
            read(k, 0).wait()
            read(k, 1).wait()
            xbuf[blk[k], rows_m, :] = (
                (1.0 - rate) * latv[k].astype(F32) + rate * noiv[k].astype(F32)
            ).astype(BF16)

    def x_own(k):
        piece = xbuf.at[blk[k], rows_m, :]
        send(rcopy(piece, piece, xs.at[0, k], xr.at[0, k], sib), home)
        send(rcopy(piece, piece, xs.at[1, k], xr.at[1, k], out), home)

    def x_event(k):
        piece = xbuf.at[blk[k], rows_o, :]

        @pl.when(home)
        def _():
            wait_on(piece, xr.at[0, k])

        @pl.when(away)
        def _():
            wait_on(piece, xr.at[1, k])

        if k % 2 == 1:
            send(rcopy(piece, piece, xs.at[2, k], xr.at[2, k], out), home)
        else:
            send(rcopy(piece, piece, xs.at[2, k], xr.at[2, k], sib), away)
        if k + 4 < 8:
            noise(k + 4)
        if k + 3 < 8:
            x_own(k + 3)

    def w_event(k, i):
        piece = wbuf.at[blk[k], w_half[i], :]
        wait_on(piece, wr.at[k, i])
        o = OFFSETS[k]
        if -3 < o <= 0 or (o == -3 and i == 0):
            send(rcopy(piece, piece, ws.at[0, k, i], wr.at[OFFSETS.index(o - 1 if o > -3 else 4), i], up_z))
        if 0 <= o < 3 or (o == 3 and i == 1):
            send(rcopy(piece, piece, ws.at[1, k, i], wr.at[OFFSETS.index(o + 1), i], dn_z))
        send(rcopy(piece, piece, wcs.at[k, i], wc.at[k, i], core_p))

    w_other = [pl.ds(pl.multiple_of((1 - c) * 320 + 160 * i, 16), 160) for i in range(2)]

    def multiply(k):
        for i in range(2):
            wait_on(wbuf.at[blk[k], w_other[i], :], wc.at[k, i])

        @pl.when(away)
        def _():
            wait_on(xbuf.at[blk[k], rows_m, :], xr.at[2, k])

        for lo, hi in ((0, 640), (640, 1152)):
            part = dot(xbuf[blk[k]], wbuf[blk[k], :, lo:hi], ((1,), (0,)))
            if k == 0:
                acc[:, lo:hi] = part
            else:
                acc[:, lo:hi] += part

    def turned(k):
        @pl.when(blk[k] // 4 == m)
        def _():
            base = lax.rem(blk[k], 4) * 320
            for i in range(5):
                t = xbuf[blk[k], :, i * 128 : (i + 1) * 128].T
                r = i * 128
                while r < (i + 1) * 128:
                    end = min((i + 1) * 128, (r // 160 + 1) * 160)
                    first = pl.multiple_of(base + (r // 320) * 160 + r % 160, 16)
                    xts[(r % 320) // 160, pl.ds(first, end - r), :] = t[r - i * 128 : end - i * 128, :]
                    r = end

    def turned_send(k):
        span = pl.ds(pl.multiple_of(lax.rem(blk[k], 4) * 320, 16), 320)
        q = lax.rem(blk[k], 4)
        send(
            rcopy(xts.at[1 - c, span, :], xto.at[span, :], xtss.at[q], xtr.at[q], core_p),
            blk[k] // 4 == m,
        )

    noise(0)
    noise(1)
    x_own(0)
    noise(2)
    x_own(1)
    noise(3)
    x_own(2)
    w_event(0, 0)
    w_event(0, 1)
    x_event(0)
    x_event(1)
    w_event(1, 0)
    w_event(2, 0)
    x_event(2)
    w_event(1, 1)
    w_event(2, 1)
    multiply(0)
    turned(0)
    x_event(3)
    w_event(3, 0)
    w_event(4, 0)
    multiply(1)
    turned_send(0)
    turned(1)
    x_event(4)
    w_event(3, 1)
    w_event(4, 1)
    multiply(2)
    turned_send(1)
    turned(2)
    x_event(5)
    w_event(5, 0)
    w_event(6, 0)
    multiply(3)
    turned_send(2)
    turned(3)
    x_event(6)
    w_event(5, 1)
    w_event(6, 1)
    multiply(4)
    turned_send(3)
    turned(4)
    x_event(7)
    multiply(5)
    turned_send(4)
    turned(5)
    multiply(6)
    turned_send(5)
    turned(6)
    w_event(7, 0)
    w_event(7, 1)
    multiply(7)
    turned_send(6)
    turned(7)
    tri[...] = acc[...].astype(BF16)
    turned_send(7)

    wait_on(gib, usem.at[3])
    wait_on(upb, usem.at[1])
    gcol[...] = jnp.transpose(jnp.broadcast_to(gib[0:1, :], (128, 512)))
    scale = 1.0 / math.sqrt(HEAD)
    fake = m == 1
    for h in range(3):
        qc, kc, vc = (pl.ds(j * 384 + h * 128, 128) for j in range(3))
        hc = pl.ds(h * 128, 128)
        for b in range(4):
            nk = min(512, (b + 2) * 128)
            rows = pl.ds(b * 128, 128)
            s = dot(tri[rows, qc], tri[0:nk, kc], ((1,), (1,))) * scale
            mine = gcol[rows, :]
            visible = gib[0:1, 0:nk] <= jnp.concatenate([mine] * (nk // 128), axis=1)
            s = jnp.where(visible, s, F32(-1e30))
            w = jnp.exp(s - jnp.max(s, axis=-1, keepdims=True))
            p = w * (1.0 / jnp.sum(w, axis=-1, keepdims=True))
            low = p.astype(BF16)
            attb[rows, hc] = dot(low, tri[0:nk, vc], ((1,), (0,))).astype(BF16)

            @pl.when(fake)
            def _():
                dp = dot(upb[rows, hc], tri[0:nk, vc], ((1,), (1,)))
                inner = jnp.sum(p * dp, axis=-1, keepdims=True)
                ds = (p * (dp - inner) * scale).astype(BF16)
                cotb[rows, qc] = dot(ds, tri[0:nk, kc], ((1,), (0,))).astype(BF16)
                pbuf[rows, 0:nk] = low
                dsbuf[rows, 0:nk] = ds

        @pl.when(fake)
        def _():
            for b in range(4):
                first = max(0, (b - 1) * 128)
                rows = pl.ds(first, 512 - first)
                keys = pl.ds(b * 128, 128)
                cotb[keys, vc] = dot(pbuf[rows, keys], upb[rows, hc], ((0,), (0,))).astype(BF16)
                cotb[keys, kc] = dot(dsbuf[rows, keys], tri[rows, qc], ((0,), (0,))).astype(BF16)

    parts = (
        (pl.ds(384, 256), sib),
        (pl.ds(640, 128), out),
        (pl.ds(768, 384), out),
        (pl.ds(0, 384), sib),
    )
    for n, (cols, peer) in enumerate(parts):
        piece = cotb.at[:, cols]
        send(rcopy(piece, piece, cs.at[n], cr.at[n], peer), fake)

    mine_cols = pl.ds(pl.multiple_of((x * 2 + yh) * 384, 128), 384)
    for dm in range(2):
        for dx in range(4):
            for dc in range(2):
                tm, tx, tc = lax.rem(m + dm, 2), lax.rem(x + dx, nx), lax.rem(c + dc, 2)
                src = attb.at[pl.ds(pl.multiple_of((tm * 8 + tx * 2 + tc) * 32, 32), 32), :]
                dst = dbuf.at[m, :, mine_cols]
                sem = dr.at[dm, dx, yh]
                cp = rcopy(src, dst, dsm.at[dm, dx, dc], sem, at(m=tm, x=tx, c=tc, yh=c))
                if dm + dx + dc == 0:
                    send(cp, away)

                    @pl.when(home)
                    def _():
                        pltpu.make_async_copy(src, dst, sem).start()
                else:
                    send(cp)

    def exchange(g):
        piece = cotb.at[:, pl.ds(g * 384, 384)]
        send(rcopy(piece, coto.at[:, pl.ds(g * 384, 384)], es.at[g], er.at[g], core_p))

    def arrived(*numbers):
        @pl.when(m == 0)
        def _():
            for n in numbers:
                wait_on(cotb.at[:, parts[n][0]], cr.at[n])

    def partials(g):
        cols = pl.ds(g * 384, 384)
        wait_on(coto.at[:, cols], er.at[g])
        for r in range(2):
            rows = pl.ds(r * 640, 640)
            gbuf[g, rows, :] = dot(xts[c, rows, :], cotb[:, cols], ((1,), (0,))) + dot(
                xto[rows, :], coto[:, cols], ((1,), (0,))
            )

    def dest(o):
        return pl.multiple_of(lax.rem(z + nz + o, nz) * 160, 16)

    def span_of(d, k):
        return pl.ds(80 * d, 80) if k == 0 else pl.ds(0, 160)

    def ring(g, k):
        for d in range(2):
            o = (4 - k) if d == 0 else (k - 4)
            first = dest(o)
            own = 80 * d
            if k >= 1:
                wait_on(rbuf.at[d, g, k - 1, span_of(d, k - 1), :], rr.at[d, g, k - 1])
            if k == 0:
                sbuf[d, g, k, own : own + 80, :] = gbuf[g, pl.ds(first + own, 80), :].astype(BF16)
            elif k == 1:
                rest = 80 - own
                sbuf[d, g, k, own : own + 80, :] = (
                    gbuf[g, pl.ds(first + own, 80), :] + rbuf[d, g, 0, own : own + 80, :].astype(F32)
                ).astype(BF16)
                sbuf[d, g, k, rest : rest + 80, :] = gbuf[g, pl.ds(first + rest, 80), :].astype(BF16)
            else:
                sbuf[d, g, k, :, :] = (
                    gbuf[g, pl.ds(first, 160), :] + rbuf[d, g, k - 1, :, :].astype(F32)
                ).astype(BF16)
        for d in range(2):
            piece = sbuf.at[d, g, k, span_of(d, k), :]
            send(
                rcopy(
                    piece, rbuf.at[d, g, k, span_of(d, k), :],
                    rs.at[d, g, k], rr.at[d, g, k], up_z if d == 0 else dn_z,
                )
            )

    def finish(g):
        for d in range(2):
            wait_on(rbuf.at[d, g, 3], rr.at[d, g, 3])
        fbuf[g] = (
            gbuf[g, pl.ds(dest(0), 160), :]
            + (rbuf[0, g, 3].astype(F32) + rbuf[1, g, 3].astype(F32))
        ).astype(BF16)

    final_parts = ((1, 0, 256, False), (1, 256, 128, True), (2, 0, 384, True), (0, 0, 384, False))

    def deliver(g):
        for n, (pg, lo, width, crossed) in enumerate(final_parts):
            if pg != g:
                continue
            piece = fbuf.at[g, :, pl.ds(lo, width)]
            dst = obuf.at[g, :, pl.ds(lo, width)]
            straight = jnp.logical_or(m == 1, not crossed)
            send(rcopy(piece, dst, fs.at[n, 0], fr.at[n], turn), jnp.logical_and(straight, away))

            @pl.when(jnp.logical_and(straight, home))
            def _():
                pltpu.make_async_copy(piece, dst, fr.at[n]).start()

            if crossed:
                send(rcopy(piece, dst, fs.at[n, 1], fr.at[n], at(c=1 - yh, yh=c)), m == 0)

    def direction():
        for dm in range(2):
            for dx in range(4):
                for b in range(2):
                    wait_on(
                        dbuf.at[lax.rem(m + dm, 2), :, pl.ds(pl.multiple_of((lax.rem(x + nx - dx, nx) * 2 + b) * 384, 128), 384)],
                        dr.at[dm, dx, b],
                    )
        dir_ref[...] = (dbuf[1].astype(F32) - dbuf[0].astype(F32)).astype(BF16)

    for q in range(4):
        wait_on(xto.at[pl.ds(q * 320, 320), :], xtr.at[q])
    arrived(0, 1)
    exchange(1)
    partials(1)
    ring(1, 0)
    arrived(2)
    exchange(2)
    partials(2)
    ring(1, 1)
    ring(2, 0)
    arrived(3)
    exchange(0)
    partials(0)
    ring(1, 2)
    ring(2, 1)
    ring(0, 0)
    direction()
    ring(1, 3)
    ring(2, 2)
    ring(0, 1)
    finish(1)
    deliver(1)
    ring(2, 3)
    ring(0, 2)
    finish(2)
    deliver(2)
    ring(0, 3)
    finish(0)
    deliver(0)
    for n, (g, lo, width, crossed) in enumerate(final_parts):
        wait_on(obuf.at[g, :, pl.ds(lo, width)], fr.at[n])
    grad_ref[...] = obuf[...]
    for cp, cond in pending:
        if cond is None:
            cp.wait_send()
        else:
            pl.when(cond)(cp.wait_send)


def per_device(latents, noise, noise_level, group_index, projections, upstream):
    weights = jnp.transpose(projections[0], (1, 0, 2))
    groups = jnp.broadcast_to(group_index, (8, group_index.shape[1]))
    dma = pltpu.SemaphoreType.DMA
    vmem = pltpu.VMEM
    anywhere = pl.BlockSpec(memory_space=pl.ANY)
    direction, grads = pl.pallas_call(
        step_kernel,
        out_shape=(
            jax.ShapeDtypeStruct((32, 3072), BF16),
            jax.ShapeDtypeStruct((3, 160, 384), BF16),
        ),
        in_specs=[anywhere, anywhere, pl.BlockSpec(memory_space=pltpu.SMEM), anywhere, anywhere, anywhere],
        out_specs=(pl.BlockSpec(memory_space=pltpu.VMEM), pl.BlockSpec(memory_space=pltpu.VMEM)),
        scratch_shapes=[
            vmem((8, 640, 1152), BF16),
            vmem((8, 512, 640), BF16),
            vmem((8, 256, 640), BF16),
            vmem((8, 256, 640), BF16),
            vmem((512, 1152), F32),
            vmem((512, 1152), BF16),
            vmem((512, 384), BF16),
            vmem((8, 512), jnp.int32),
            vmem((512, 128), jnp.int32),
            vmem((512, 384), BF16),
            vmem((512, 1152), BF16),
            vmem((512, 1152), BF16),
            vmem((2, 1280, 512), BF16),
            vmem((1280, 512), BF16),
            vmem((512, 512), BF16),
            vmem((512, 512), BF16),
            vmem((3, 1280, 384), F32),
            vmem((2, 3, 4, 160, 384), BF16),
            vmem((2, 3, 4, 160, 384), BF16),
            vmem((3, 160, 384), BF16),
            vmem((3, 160, 384), BF16),
            vmem((2, 32, 3072), BF16),
            dma((8, 2)), dma((8, 2)), dma((2, 8, 2)), dma((8, 2)), dma((2, 3)),
            dma((3, 8)), dma((3, 8)), dma((8, 2)), dma((4,)), dma((4,)), dma((4,)),
            dma((4,)), dma((4,)), dma((3,)), dma((3,)),
            dma((2, 3, 4)), dma((2, 3, 4)), dma((4,)), dma((4, 2)),
            dma((2, 4, 2)), dma((2, 4, 2)),
        ],
        compiler_params=pltpu.CompilerParams(
            collective_id=0, has_side_effects=True, vmem_limit_bytes=62 << 20
        ),
    )(latents[0], noise[0], noise_level, weights, upstream[0], groups)
    grads = jnp.transpose(grads.astype(F32), (1, 0, 2))
    return direction[None], grads


def solution(mesh):
    split = Mesh(
        mesh.devices.reshape(2, mesh.shape["seq"] // 2, 2, mesh.shape["fsdp"] // 2, 2), AXES
    )
    clip, heads = ("z", "yh"), ("x", "c")
    return jax.shard_map(
        step_kernel_call,
        mesh=split,
        in_specs=(
            P(clip, "m", None),
            P(clip, "m", None),
            P(clip),
            P(clip, None),
            P("m", clip, None, heads),
            P(clip, None, heads),
        ),
        out_specs=(P(clip, ("m", "x", "c"), None), P(("m", "z", "yh"), None, heads)),
        check_vma=False,
    )


step_kernel_call = per_device
```

```python
import math

import jax
import jax.numpy as jnp
from jax import lax
from jax.experimental import pallas as pl
from jax.experimental.pallas import tpu as pltpu
from jax.sharding import Mesh
from jax.sharding import PartitionSpec as P

HEAD = 128
AXES = ("m", "x", "c", "z", "yh")
MESH_ID = pl.DeviceIdType.MESH
F32 = jnp.float32
BF16 = jnp.bfloat16
OFFSETS = (0, -1, 1, -2, 2, -3, 3, 4)


def dot(a, b, dims):
    return lax.dot_general(a, b, (dims, ((), ())), preferred_element_type=F32)


def step_kernel(
    lat_ref, noi_ref, lvl_ref, proj_ref, up_ref, gi_ref,
    dir_ref, grad_ref,
    wbuf, xbuf, latv, noiv, acc, tri, upb, gib, gcol, attb, cotb, coto,
    xts, xto, pbuf, dsbuf, gbuf, sbuf, rbuf, fbuf, obuf, dbuf,
    wr, wc, ws, wcs, wos, xr, xs, lsem, usem, xtr, xtss, cr, cs, er, es,
    rr, rs, fr, fs, dr, dsm,
):
    m, x, c, z, yh = (lax.axis_index(a) for a in AXES)
    nz = lax.axis_size("z")
    nx = lax.axis_size("x")
    home = c == yh
    away = c != yh

    def at(**k):
        return k

    core_p = at(c=1 - c)
    sib = at(m=1 - m)
    out = at(m=1 - m, yh=1 - yh)
    turn = at(c=yh, yh=c)
    up_z = at(z=lax.rem(z + 1, nz))
    dn_z = at(z=lax.rem(z + nz - 1, nz))
    blk = [lax.rem(z + nz + o, nz) for o in OFFSETS]

    def rcopy(src, dst, ss, rsem, dev):
        return pltpu.make_async_remote_copy(
            src_ref=src, dst_ref=dst, send_sem=ss, recv_sem=rsem,
            device_id=dev, device_id_type=MESH_ID,
        )

    def wait_on(ref, sem):
        pltpu.make_async_copy(ref, ref, sem).wait()

    pending = []

    def send(cp, cond=None):
        if cond is None:
            cp.start()
        else:
            pl.when(cond)(cp.start)
        pending.append((cp, cond))

    rows_m = pl.ds(pl.multiple_of(m * 256, 256), 256)
    rows_o = pl.ds(pl.multiple_of((1 - m) * 256, 256), 256)

    def lane(k):
        return pl.ds(pl.multiple_of(blk[k] * 640, 128), 640)

    def read(k, which):
        src, dst = ((lat_ref, latv), (noi_ref, noiv))[which]
        return pltpu.make_async_copy(src.at[:, lane(k)], dst.at[k], lsem.at[k, which])

    w_half = [pl.ds(pl.multiple_of(c * 320 + 160 * i, 16), 160) for i in range(2)]
    w_home = [pl.ds(pl.multiple_of(yh * 320 + 160 * i, 16), 160) for i in range(2)]

    @pl.when(home)
    def _():
        for i in range(2):
            for j in range(3):
                pltpu.make_async_copy(
                    proj_ref.at[j, pl.ds(160 * i, 160), :],
                    wbuf.at[z, w_home[i], pl.ds(384 * j, 384)], wr.at[0, i],
                ).start()
        for k in range(8):
            read(k, 0).start()
            read(k, 1).start()

    barrier = pltpu.get_barrier_semaphore()
    count = 0
    for dm in range(2):
        for dx in range(4):
            for dc in range(2):
                for dy in range(2):
                    if dm + dx + dc + dy == 0:
                        continue
                    peer = at(
                        m=lax.rem(m + dm, 2), x=lax.rem(x + dx, nx),
                        c=lax.rem(c + dc, 2), yh=lax.rem(yh + dy, 2),
                    )
                    pl.semaphore_signal(barrier, inc=1, device_id=peer, device_id_type=MESH_ID)
                    count += 1
    for peer in (up_z, dn_z):
        pl.semaphore_signal(barrier, inc=1, device_id=peer, device_id_type=MESH_ID)
        count += 1
    pl.semaphore_wait(barrier, count)

    for i in range(2):
        for j in range(3):
            send(
                rcopy(
                    proj_ref.at[j, pl.ds(160 * i, 160), :],
                    wbuf.at[z, w_home[i], pl.ds(384 * j, 384)],
                    wos.at[i, j], wr.at[0, i], turn,
                ),
                away,
            )
    send(rcopy(gi_ref, gib, usem.at[2], usem.at[3], turn), away)
    up_keep = jnp.logical_or(home, m == 0)
    up_move = jnp.logical_and(away, m == 1)
    send(rcopy(up_ref, upb, usem.at[0], usem.at[1], turn), up_move)

    @pl.when(up_keep)
    def _():
        pltpu.make_async_copy(up_ref, upb, usem.at[1]).start()

    @pl.when(home)
    def _():
        pltpu.make_async_copy(gi_ref, gib, usem.at[3]).start()

    rate = lvl_ref[0]

    def noise(k):
        @pl.when(home)
        def _():
            read(k, 0).wait()
            read(k, 1).wait()
            xbuf[blk[k], rows_m, :] = (
                (1.0 - rate) * latv[k].astype(F32) + rate * noiv[k].astype(F32)
            ).astype(BF16)

    def x_own(k):
        piece = xbuf.at[blk[k], rows_m, :]
        send(rcopy(piece, piece, xs.at[0, k], xr.at[0, k], sib), home)
        send(rcopy(piece, piece, xs.at[1, k], xr.at[1, k], out), home)

    def x_event(k):
        piece = xbuf.at[blk[k], rows_o, :]

        @pl.when(home)
        def _():
            wait_on(piece, xr.at[0, k])

        @pl.when(away)
        def _():
            wait_on(piece, xr.at[1, k])

        if k % 2 == 1:
            send(rcopy(piece, piece, xs.at[2, k], xr.at[2, k], out), home)
        else:
            send(rcopy(piece, piece, xs.at[2, k], xr.at[2, k], sib), away)
        if k + 4 < 8:
            noise(k + 4)
        if k + 3 < 8:
            x_own(k + 3)

    def w_event(k, i):
        piece = wbuf.at[blk[k], w_half[i], :]
        wait_on(piece, wr.at[k, i])
        o = OFFSETS[k]
        if -3 < o <= 0 or (o == -3 and i == 0):
            send(rcopy(piece, piece, ws.at[0, k, i], wr.at[OFFSETS.index(o - 1 if o > -3 else 4), i], up_z))
        if 0 <= o < 3 or (o == 3 and i == 1):
            send(rcopy(piece, piece, ws.at[1, k, i], wr.at[OFFSETS.index(o + 1), i], dn_z))
        send(rcopy(piece, piece, wcs.at[k, i], wc.at[k, i], core_p))

    w_other = [pl.ds(pl.multiple_of((1 - c) * 320 + 160 * i, 16), 160) for i in range(2)]

    def multiply(k):
        for i in range(2):
            wait_on(wbuf.at[blk[k], w_other[i], :], wc.at[k, i])

        @pl.when(away)
        def _():
            wait_on(xbuf.at[blk[k], rows_m, :], xr.at[2, k])

        for lo, hi in ((0, 640), (640, 1152)):
            part = dot(xbuf[blk[k]], wbuf[blk[k], :, lo:hi], ((1,), (0,)))
            if k == 0:
                acc[:, lo:hi] = part
            else:
                acc[:, lo:hi] += part

    def turned(k):
        @pl.when(blk[k] // 4 == m)
        def _():
            base = lax.rem(blk[k], 4) * 320
            for i in range(5):
                t = xbuf[blk[k], :, i * 128 : (i + 1) * 128].T
                r = i * 128
                while r < (i + 1) * 128:
                    end = min((i + 1) * 128, (r // 160 + 1) * 160)
                    first = pl.multiple_of(base + (r // 320) * 160 + r % 160, 16)
                    xts[(r % 320) // 160, pl.ds(first, end - r), :] = t[r - i * 128 : end - i * 128, :]
                    r = end

    def turned_send(k):
        span = pl.ds(pl.multiple_of(lax.rem(blk[k], 4) * 320, 16), 320)
        q = lax.rem(blk[k], 4)
        send(
            rcopy(xts.at[1 - c, span, :], xto.at[span, :], xtss.at[q], xtr.at[q], core_p),
            blk[k] // 4 == m,
        )

    noise(0)
    noise(1)
    x_own(0)
    noise(2)
    x_own(1)
    noise(3)
    x_own(2)
    w_event(0, 0)
    w_event(0, 1)
    x_event(0)
    x_event(1)
    w_event(1, 0)
    w_event(2, 0)
    x_event(2)
    w_event(1, 1)
    w_event(2, 1)
    multiply(0)
    turned(0)
    x_event(3)
    w_event(3, 0)
    w_event(4, 0)
    multiply(1)
    turned_send(0)
    turned(1)
    x_event(4)
    w_event(3, 1)
    w_event(4, 1)
    multiply(2)
    turned_send(1)
    turned(2)
    x_event(5)
    w_event(5, 0)
    w_event(6, 0)
    multiply(3)
    turned_send(2)
    turned(3)
    x_event(6)
    w_event(5, 1)
    w_event(6, 1)
    multiply(4)
    turned_send(3)
    turned(4)
    x_event(7)
    multiply(5)
    turned_send(4)
    turned(5)
    multiply(6)
    turned_send(5)
    turned(6)
    w_event(7, 0)
    w_event(7, 1)
    multiply(7)
    turned_send(6)
    turned(7)
    tri[...] = acc[...].astype(BF16)
    turned_send(7)

    wait_on(gib, usem.at[3])
    wait_on(upb, usem.at[1])
    gcol[...] = jnp.transpose(jnp.broadcast_to(gib[0:1, :], (128, 512)))
    scale = 1.0 / math.sqrt(HEAD)
    fake = m == 1
    def attend(h):
        qc, kc, vc = (pl.ds(j * 384 + h * 128, 128) for j in range(3))
        dq, dk, dv = (pl.ds(h * 384 + j * 128, 128) for j in range(3))
        hc = pl.ds(h * 128, 128)
        for b in range(4):
            nk = min(512, (b + 2) * 128)
            rows = pl.ds(b * 128, 128)
            s = dot(tri[rows, qc], tri[0:nk, kc], ((1,), (1,))) * scale
            mine = gcol[rows, :]
            visible = gib[0:1, 0:nk] <= jnp.concatenate([mine] * (nk // 128), axis=1)
            s = jnp.where(visible, s, F32(-1e30))
            w = jnp.exp(s - jnp.max(s, axis=-1, keepdims=True))
            p = w * (1.0 / jnp.sum(w, axis=-1, keepdims=True))
            low = p.astype(BF16)
            attb[rows, hc] = dot(low, tri[0:nk, vc], ((1,), (0,))).astype(BF16)

            @pl.when(fake)
            def _():
                dp = dot(upb[rows, hc], tri[0:nk, vc], ((1,), (1,)))
                inner = jnp.sum(p * dp, axis=-1, keepdims=True)
                ds = (p * (dp - inner) * scale).astype(BF16)
                cotb[rows, dq] = dot(ds, tri[0:nk, kc], ((1,), (0,))).astype(BF16)
                pbuf[rows, 0:nk] = low
                dsbuf[rows, 0:nk] = ds

        @pl.when(fake)
        def _():
            for b in range(4):
                first = max(0, (b - 1) * 128)
                rows = pl.ds(first, 512 - first)
                keys = pl.ds(b * 128, 128)
                cotb[keys, dv] = dot(pbuf[rows, keys], upb[rows, hc], ((0,), (0,))).astype(BF16)
                cotb[keys, dk] = dot(dsbuf[rows, keys], tri[rows, qc], ((0,), (0,))).astype(BF16)

    split_at = (256, 128, 256)

    def part(g, n):
        lo, hi = ((0, split_at[g]), (split_at[g], 384))[n]
        return pl.ds(g * 384 + lo, hi - lo)

    def spread(g):
        for n, peer in ((0, sib), (1, out)):
            piece = cotb.at[:, part(g, n)]
            send(rcopy(piece, piece, cs.at[g, n], cr.at[g, n], peer), fake)

    mine_cols = pl.ds(pl.multiple_of((x * 2 + yh) * 384, 128), 384)

    def direction_send(dm, dx):
            for dc in range(2):
                tm, tx, tc = lax.rem(m + dm, 2), lax.rem(x + dx, nx), lax.rem(c + dc, 2)
                src = attb.at[pl.ds(pl.multiple_of((tm * 8 + tx * 2 + tc) * 32, 32), 32), :]
                dst = dbuf.at[m, :, mine_cols]
                sem = dr.at[dm, dx, yh]
                cp = rcopy(src, dst, dsm.at[dm, dx, dc], sem, at(m=tm, x=tx, c=tc, yh=c))
                if dm + dx + dc == 0:
                    send(cp, away)

                    @pl.when(home)
                    def _():
                        pltpu.make_async_copy(src, dst, sem).start()
                else:
                    send(cp)

    def exchange(g, cond):
        piece = cotb.at[:, pl.ds(g * 384, 384)]
        send(rcopy(piece, coto.at[:, pl.ds(g * 384, 384)], es.at[g], er.at[g], core_p), cond)

    def arrived(g):
        @pl.when(m == 0)
        def _():
            for n in range(2):
                wait_on(cotb.at[:, part(g, n)], cr.at[g, n])

    def partials(g):
        cols = pl.ds(g * 384, 384)
        wait_on(coto.at[:, cols], er.at[g])
        for r in range(2):
            rows = pl.ds(r * 640, 640)
            gbuf[g, rows, :] = dot(xts[c, rows, :], cotb[:, cols], ((1,), (0,))) + dot(
                xto[rows, :], coto[:, cols], ((1,), (0,))
            )

    def dest(o):
        return pl.multiple_of(lax.rem(z + nz + o, nz) * 160, 16)

    def span_of(d, k):
        return pl.ds(80 * d, 80) if k == 0 else pl.ds(0, 160)

    def ring(g, k):
        for d in range(2):
            o = (4 - k) if d == 0 else (k - 4)
            first = dest(o)
            own = 80 * d
            if k >= 1:
                wait_on(rbuf.at[d, g, k - 1, span_of(d, k - 1), :], rr.at[d, g, k - 1])
            if k == 0:
                sbuf[d, g, k, own : own + 80, :] = gbuf[g, pl.ds(first + own, 80), :].astype(BF16)
            elif k == 1:
                rest = 80 - own
                sbuf[d, g, k, own : own + 80, :] = (
                    gbuf[g, pl.ds(first + own, 80), :] + rbuf[d, g, 0, own : own + 80, :].astype(F32)
                ).astype(BF16)
                sbuf[d, g, k, rest : rest + 80, :] = gbuf[g, pl.ds(first + rest, 80), :].astype(BF16)
            else:
                sbuf[d, g, k, :, :] = (
                    gbuf[g, pl.ds(first, 160), :] + rbuf[d, g, k - 1, :, :].astype(F32)
                ).astype(BF16)
        for d in range(2):
            piece = sbuf.at[d, g, k, span_of(d, k), :]
            send(
                rcopy(
                    piece, rbuf.at[d, g, k, span_of(d, k), :],
                    rs.at[d, g, k], rr.at[d, g, k], up_z if d == 0 else dn_z,
                )
            )

    def finish(g):
        for d in range(2):
            wait_on(rbuf.at[d, g, 3], rr.at[d, g, 3])
        fbuf[g] = (
            gbuf[g, pl.ds(dest(0), 160), :]
            + (rbuf[0, g, 3].astype(F32) + rbuf[1, g, 3].astype(F32))
        ).astype(BF16)

    def deliver(g):
        for n, (lo, hi) in enumerate(((0, split_at[g]), (split_at[g], 384))):
            piece = fbuf.at[g, :, pl.ds(lo, hi - lo)]
            dst = obuf.at[g, :, pl.ds(lo, hi - lo)]
            straight = jnp.logical_or(m == 1, n == 0)
            send(rcopy(piece, dst, fs.at[g, n, 0], fr.at[g, n], turn), jnp.logical_and(straight, away))

            @pl.when(jnp.logical_and(straight, home))
            def _():
                pltpu.make_async_copy(piece, dst, fr.at[g, n]).start()

            if n == 1:
                send(rcopy(piece, dst, fs.at[g, n, 1], fr.at[g, n], at(c=1 - yh, yh=c)), m == 0)

    def direction():
        for dm in range(2):
            for dx in range(4):
                for b in range(2):
                    wait_on(
                        dbuf.at[lax.rem(m + dm, 2), :, pl.ds(pl.multiple_of((lax.rem(x + nx - dx, nx) * 2 + b) * 384, 128), 384)],
                        dr.at[dm, dx, b],
                    )
        dir_ref[...] = (dbuf[1].astype(F32) - dbuf[0].astype(F32)).astype(BF16)

    def shared(g):
        arrived(g)
        exchange(g, m == 0)

    attend(0)
    spread(0)
    exchange(0, fake)
    attend(1)
    spread(1)
    exchange(1, fake)
    for q in range(4):
        wait_on(xto.at[pl.ds(q * 320, 320), :], xtr.at[q])
    shared(0)
    partials(0)
    ring(0, 0)
    attend(2)
    spread(2)
    exchange(2, fake)
    shared(1)
    partials(1)
    ring(0, 1)
    ring(1, 0)
    for dm in range(2):
        for dx in range(4):
            direction_send(dm, dx)
    shared(2)
    partials(2)
    ring(0, 2)
    ring(1, 1)
    ring(2, 0)
    ring(0, 3)
    ring(1, 2)
    ring(2, 1)
    finish(0)
    deliver(0)
    ring(1, 3)
    ring(2, 2)
    finish(1)
    deliver(1)
    ring(2, 3)
    direction()
    finish(2)
    deliver(2)
    for g in range(3):
        for n in range(2):
            lo, hi = ((0, split_at[g]), (split_at[g], 384))[n]
            wait_on(obuf.at[g, :, pl.ds(lo, hi - lo)], fr.at[g, n])
        for j in range(3):
            grad_ref[j, :, pl.ds(g * 128, 128)] = obuf[g, :, pl.ds(j * 128, 128)]
    for cp, cond in pending:
        if cond is None:
            cp.wait_send()
        else:
            pl.when(cond)(cp.wait_send)


def per_device(latents, noise, noise_level, group_index, projections, upstream):
    weights = jnp.transpose(projections[0], (1, 0, 2))
    groups = jnp.broadcast_to(group_index, (8, group_index.shape[1]))
    dma = pltpu.SemaphoreType.DMA
    vmem = pltpu.VMEM
    anywhere = pl.BlockSpec(memory_space=pl.ANY)
    direction, grads = pl.pallas_call(
        step_kernel,
        out_shape=(
            jax.ShapeDtypeStruct((32, 3072), BF16),
            jax.ShapeDtypeStruct((3, 160, 384), BF16),
        ),
        in_specs=[anywhere, anywhere, pl.BlockSpec(memory_space=pltpu.SMEM), anywhere, anywhere, anywhere],
        out_specs=(pl.BlockSpec(memory_space=pltpu.VMEM), pl.BlockSpec(memory_space=pltpu.VMEM)),
        scratch_shapes=[
            vmem((8, 640, 1152), BF16),
            vmem((8, 512, 640), BF16),
            vmem((8, 256, 640), BF16),
            vmem((8, 256, 640), BF16),
            vmem((512, 1152), F32),
            vmem((512, 1152), BF16),
            vmem((512, 384), BF16),
            vmem((8, 512), jnp.int32),
            vmem((512, 128), jnp.int32),
            vmem((512, 384), BF16),
            vmem((512, 1152), BF16),
            vmem((512, 1152), BF16),
            vmem((2, 1280, 512), BF16),
            vmem((1280, 512), BF16),
            vmem((512, 512), BF16),
            vmem((512, 512), BF16),
            vmem((3, 1280, 384), F32),
            vmem((2, 3, 4, 160, 384), BF16),
            vmem((2, 3, 4, 160, 384), BF16),
            vmem((3, 160, 384), BF16),
            vmem((3, 160, 384), BF16),
            vmem((2, 32, 3072), BF16),
            dma((8, 2)), dma((8, 2)), dma((2, 8, 2)), dma((8, 2)), dma((2, 3)),
            dma((3, 8)), dma((3, 8)), dma((8, 2)), dma((4,)), dma((4,)), dma((4,)),
            dma((3, 2)), dma((3, 2)), dma((3,)), dma((3,)),
            dma((2, 3, 4)), dma((2, 3, 4)), dma((3, 2)), dma((3, 2, 2)),
            dma((2, 4, 2)), dma((2, 4, 2)),
        ],
        compiler_params=pltpu.CompilerParams(
            collective_id=0, has_side_effects=True, vmem_limit_bytes=62 << 20
        ),
    )(latents[0], noise[0], noise_level, weights, upstream[0], groups)
    grads = jnp.transpose(grads.astype(F32), (1, 0, 2))
    return direction[None], grads


def solution(mesh):
    split = Mesh(
        mesh.devices.reshape(2, mesh.shape["seq"] // 2, 2, mesh.shape["fsdp"] // 2, 2), AXES
    )
    clip, heads = ("z", "yh"), ("x", "c")
    return jax.shard_map(
        step_kernel_call,
        mesh=split,
        in_specs=(
            P(clip, "m", None),
            P(clip, "m", None),
            P(clip),
            P(clip, None),
            P("m", clip, None, heads),
            P(clip, None, heads),
        ),
        out_specs=(P(clip, ("m", "x", "c"), None), P(("m", "z", "yh"), None, heads)),
        check_vma=False,
    )


step_kernel_call = per_device
```

```python
import math

import jax
import jax.numpy as jnp
from jax import lax
from jax.experimental import pallas as pl
from jax.experimental.pallas import tpu as pltpu
from jax.sharding import Mesh
from jax.sharding import PartitionSpec as P

HEAD = 128
AXES = ("m", "x", "c", "z", "yh")
MESH_ID = pl.DeviceIdType.MESH
F32 = jnp.float32
BF16 = jnp.bfloat16
OFFSETS = (0, -1, 1, -2, 2, -3, 3, 4)


def dot(a, b, dims):
    return lax.dot_general(a, b, (dims, ((), ())), preferred_element_type=F32)


def step_kernel(
    lat_ref, noi_ref, lvl_ref, proj_ref, up_ref, gi_ref,
    dir_ref, grad_ref,
    wbuf, xbuf, latv, noiv, acc, tri, upb, gib, gcol, attb, cotb, coto,
    xts, xto, pbuf, dsbuf, gbuf, sbuf, rbuf, fbuf, obuf, dbuf,
    wr, wc, ws, wcs, wos, ya, xa, xs, xxs, lsem, usem, xtr, xtss, cr, cs, er, es,
    rr, rs, fr, fs, dr, dsm,
):
    m, x, c, z, yh = (lax.axis_index(a) for a in AXES)
    nz = lax.axis_size("z")
    nx = lax.axis_size("x")
    home = c == yh
    away = c != yh

    def at(**k):
        return k

    core_p = at(c=1 - c)
    sib = at(m=1 - m)
    out = at(m=1 - m, yh=1 - yh)
    turn = at(c=yh, yh=c)
    up_z = at(z=lax.rem(z + 1, nz))
    dn_z = at(z=lax.rem(z + nz - 1, nz))
    blk = [lax.rem(z + nz + o, nz) for o in OFFSETS]

    def rcopy(src, dst, ss, rsem, dev):
        return pltpu.make_async_remote_copy(
            src_ref=src, dst_ref=dst, send_sem=ss, recv_sem=rsem,
            device_id=dev, device_id_type=MESH_ID,
        )

    def wait_on(ref, sem):
        pltpu.make_async_copy(ref, ref, sem).wait()

    pending = []

    def go(cp, cond=None):
        if cond is None:
            cp.start()
        else:
            pl.when(cond)(cp.start)

    def send(cp, cond=None):
        go(cp, cond)
        pending.append((cp.wait_send, cond))

    def sent(ref, sem, cond=None):
        pending.append((lambda: wait_on(ref, sem), cond))

    def settle(number):
        for wait, cond in pending[:number]:
            if cond is None:
                wait()
            else:
                pl.when(cond)(wait)
        del pending[:number]

    rows_m = pl.ds(pl.multiple_of(m * 256, 256), 256)

    def read(p, which):
        src, dst = ((lat_ref, latv), (noi_ref, noiv))[which]
        return pltpu.make_async_copy(src.at[:, pl.ds(p * 1280, 1280)], dst.at[p], lsem.at[p, which])

    def w_rows(zb, core, i):
        return pl.ds(pl.multiple_of(zb * 640 + core * 320 + i * 160, 16), 160)

    def own_rows(h, i, j):
        return (
            proj_ref.at[j, pl.ds(160 * i, 160), pl.ds(128 * h, 128)],
            wbuf.at[h, w_rows(z, yh, i), pl.ds(128 * j, 128)],
        )

    every_own = [(h, i, j) for h in range(3) for i in range(2) for j in range(3)]

    @pl.when(home)
    def _():
        for h, i, j in every_own:
            pltpu.make_async_copy(*own_rows(h, i, j), wr.at[h, 0, i]).start()
            if (i, j) == (1, 2) and h < 2:
                for p in (2 * h, 2 * h + 1):
                    read(p, 0).start()
                    read(p, 1).start()

    barrier = pltpu.get_barrier_semaphore()
    count = 0
    for dm in range(2):
        for dx in range(4):
            for dc in range(2):
                for dy in range(2):
                    if dm + dx + dc + dy == 0:
                        continue
                    peer = at(
                        m=lax.rem(m + dm, 2), x=lax.rem(x + dx, nx),
                        c=lax.rem(c + dc, 2), yh=lax.rem(yh + dy, 2),
                    )
                    pl.semaphore_signal(barrier, inc=1, device_id=peer, device_id_type=MESH_ID)
                    count += 1
    for peer in (up_z, dn_z):
        pl.semaphore_signal(barrier, inc=1, device_id=peer, device_id_type=MESH_ID)
        count += 1
    pl.semaphore_wait(barrier, count)

    def w_turn(h):
        for i in range(2):
            for j in range(3):
                src, dst = own_rows(h, i, j)
                go(rcopy(src, dst, wos.at[h], wr.at[h, 0, i], turn), away)
        sent(wbuf.at[h, 0:320, :], wos.at[h], away)

    w_turn(0)

    def side_inputs():
        send(rcopy(gi_ref, gib, usem.at[2], usem.at[3], turn), away)
        send(rcopy(up_ref, upb, usem.at[0], usem.at[1], turn), jnp.logical_and(away, m == 1))

        @pl.when(jnp.logical_or(home, m == 0))
        def _():
            pltpu.make_async_copy(up_ref, upb, usem.at[1]).start()

        @pl.when(home)
        def _():
            pltpu.make_async_copy(gi_ref, gib, usem.at[3]).start()

    rate = lvl_ref[0]

    up_x = at(x=lax.rem(x + 1, nx))
    dn_x = at(x=lax.rem(x + nx - 1, nx))

    def quarter(half, step):
        first = half * 256 + lax.rem(x + nx + step, nx) * 64
        return pl.ds(pl.multiple_of(first, 64), 64)

    def noise(p):
        @pl.when(home)
        def _():
            read(p, 0).wait()
            read(p, 1).wait()
            for lo in (0, 640):
                xbuf[p, rows_m, lo : lo + 640] = (
                    (1.0 - rate) * latv[p, :, lo : lo + 640].astype(F32)
                    + rate * noiv[p, :, lo : lo + 640].astype(F32)
                ).astype(BF16)

    def x_own(p):
        for q in range(2):
            piece = xbuf.at[p, quarter(m, q), :]
            go(rcopy(piece, piece, xs.at[p], ya.at[p, 0], sib), home)
            go(rcopy(piece, piece, xs.at[p], ya.at[p, 0], out), home)

    def x_side(p, kind, q, cond):
        piece = xbuf.at[p, quarter((1 - m) if kind == 0 else m, q), :]
        go(rcopy(piece, piece, xxs.at[p], xa.at[p, kind], up_x if q == 0 else dn_x), cond)

    def x_y(p):
        wait_on(xbuf.at[p, 0:128, :], ya.at[p, 0])
        for q in range(2):
            piece = xbuf.at[p, quarter(1 - m, q), :]
            if p % 2 == 1:
                go(rcopy(piece, piece, xs.at[p], ya.at[p, 1], out), home)
            else:
                go(rcopy(piece, piece, xs.at[p], ya.at[p, 1], sib), away)
            x_side(p, 0, q, None)

    def x_z(p):
        @pl.when(away)
        def _():
            wait_on(xbuf.at[p, 0:128, :], ya.at[p, 1])

        for q in range(2):
            x_side(p, 1, q, away)

    def x_ready(p):
        wait_on(xbuf.at[p, 0:128, :], xa.at[p, 0])

        @pl.when(away)
        def _():
            wait_on(xbuf.at[p, 0:128, :], xa.at[p, 1])

        sent(xbuf.at[p, 0 : 256 + 128 * (p % 2), :], xs.at[p], home)
        if p % 2 == 0:
            sent(xbuf.at[p, 0:128, :], xs.at[p], away)
        sent(xbuf.at[p, 0:128, :], xxs.at[p], home)
        sent(xbuf.at[p, 0:256, :], xxs.at[p], away)

    def w_event(h, k, i, cond=None):
        piece = wbuf.at[h, w_rows(blk[k], c, i), :]
        if cond is None:
            wait_on(piece, wr.at[h, k, i])
        else:
            pl.when(cond)(lambda: wait_on(piece, wr.at[h, k, i]))
        o = OFFSETS[k]
        if -3 < o <= 0 or (o == -3 and i == 0):
            to = OFFSETS.index(o - 1 if o > -3 else 4)
            go(rcopy(piece, piece, ws.at[h], wr.at[h, to, i], up_z), cond)
        if 0 <= o < 3 or (o == 3 and i == 1):
            go(rcopy(piece, piece, ws.at[h], wr.at[h, OFFSETS.index(o + 1), i], dn_z), cond)
        go(rcopy(piece, piece, wcs.at[h], wc.at[h, k], core_p), cond)

    def stage(h, n, i):
        w_event(h, 2 * n - 1, i)
        w_event(h, 2 * n, i)

    def last(h):
        w_event(h, 7, 0)
        w_event(h, 7, 1)
        sent(wbuf.at[h, 0:2240, :], ws.at[h])
        sent(wbuf.at[h, 0:2560, :], wcs.at[h])

    def w_other(h, k):
        first = pl.multiple_of(blk[k] * 640 + (1 - c) * 320, 64)
        wait_on(wbuf.at[h, pl.ds(first, 320), :], wc.at[h, k])

    def gather(first, part):
        if first:
            acc[...] = part
        else:
            acc[...] += part

    def multiply_columns(p):
        if p == 0:
            for k in range(8):
                w_other(0, k)
        gather(p == 0, dot(xbuf[p], wbuf[0, p * 1280 : (p + 1) * 1280, :], ((1,), (0,))))

    def multiply(h, *blocks):
        for k in blocks:
            w_other(h, k)
            cols = pl.ds(pl.multiple_of(lax.rem(blk[k], 2) * 640, 128), 640)
            rows = pl.ds(pl.multiple_of(blk[k] * 640, 128), 640)
            gather(k == 0, dot(xbuf[blk[k] // 2, :, cols], wbuf[h, rows, :], ((1,), (0,))))

    def keep(h):
        tri[h] = acc[...].astype(BF16)

    def turned(p):
        @pl.when(m == p // 2)
        def _():
            base = (p % 2) * 640
            for i in range(10):
                t = xbuf[p, :, i * 128 : (i + 1) * 128].T
                r = i * 128
                while r < (i + 1) * 128:
                    end = min((i + 1) * 128, (r // 160 + 1) * 160)
                    first = base + (r // 320) * 160 + r % 160
                    xts[(r % 320) // 160, pl.ds(first, end - r), :] = t[r - i * 128 : end - i * 128, :]
                    r = end

    def turned_send(p):
        span = pl.ds((p % 2) * 640, 640)
        send(
            rcopy(xts.at[1 - c, span, :], xto.at[span, :], xtss.at[p % 2], xtr.at[p % 2], core_p),
            m == p // 2,
        )

    def attention_inputs():
        wait_on(gib, usem.at[3])
        wait_on(upb, usem.at[1])
        gcol[...] = jnp.transpose(jnp.broadcast_to(gib[...], (128, 512)))

    scale = 1.0 / math.sqrt(HEAD)
    fake = m == 1
    def attend(h):
        qc, kc, vc = (pl.ds(j * 128, 128) for j in range(3))
        dq = pl.ds(h * 384, 128)
        hc = pl.ds(h * 128, 128)
        for b in range(4):
            nk = min(512, (b + 2) * 128)
            rows = pl.ds(b * 128, 128)
            s = dot(tri[h, rows, qc], tri[h, 0:nk, kc], ((1,), (1,))) * scale
            mine = gcol[rows, :]
            visible = gib[0:1, 0:nk] <= jnp.concatenate([mine] * (nk // 128), axis=1)
            s = jnp.where(visible, s, F32(-1e30))
            w = jnp.exp(s - jnp.max(s, axis=-1, keepdims=True))
            p = w * (1.0 / jnp.sum(w, axis=-1, keepdims=True))
            low = p.astype(BF16)
            attb[rows, hc] = dot(low, tri[h, 0:nk, vc], ((1,), (0,))).astype(BF16)

            @pl.when(fake)
            def _():
                dp = dot(upb[rows, hc], tri[h, 0:nk, vc], ((1,), (1,)))
                inner = jnp.sum(p * dp, axis=-1, keepdims=True)
                ds = (p * (dp - inner) * scale).astype(BF16)
                cotb[rows, dq] = dot(ds, tri[h, 0:nk, kc], ((1,), (0,))).astype(BF16)
                pbuf[rows, 0:nk] = low
                dsbuf[rows, 0:nk] = ds

    def key_side(h, j):
        left, right = (
            (dsbuf, tri.at[h, :, pl.ds(0, 128)]) if j == 1 else (pbuf, upb.at[:, pl.ds(h * 128, 128)])
        )

        @pl.when(fake)
        def _():
            for b in range(4):
                first = max(0, (b - 1) * 128)
                rows = pl.ds(first, 512 - first)
                keys = pl.ds(b * 128, 128)
                cotb[keys, pl.ds(h * 384 + j * 128, 128)] = dot(
                    left[rows, keys], right[rows, :], ((0,), (0,))
                ).astype(BF16)

    parts = (
        (0, 0, 256, False), (0, 256, 128, True),
        (1, 384, 128, False), (1, 512, 256, True),
        (2, 768, 256, False),
        (3, 1024, 128, True),
    )
    groups = ((0, 384), (384, 384), (768, 256), (1024, 128))

    def spread(g):
        for n, (pg, col, width, outer) in enumerate(parts):
            if pg == g:
                piece = cotb.at[:, pl.ds(col, width)]
                send(rcopy(piece, piece, cs.at[n], cr.at[n], out if outer else sib), fake)

    mine_cols = pl.ds(pl.multiple_of((x * 2 + yh) * 384, 128), 384)

    def direction_send():
        for dm in range(2):
            for dx in range(4):
                for dc in range(2):
                    tm, tx, tc = lax.rem(m + dm, 2), lax.rem(x + dx, nx), lax.rem(c + dc, 2)
                    src = attb.at[pl.ds(pl.multiple_of((tm * 8 + tx * 2 + tc) * 32, 32), 32), :]
                    dst = dbuf.at[m, :, mine_cols]
                    sem = dr.at[dm, dx, yh]
                    cp = rcopy(src, dst, dsm, sem, at(m=tm, x=tx, c=tc, yh=c))
                    if dm + dx + dc == 0:
                        go(cp, away)

                        @pl.when(home)
                        def _():
                            pltpu.make_async_copy(src, dst, sem).start()
                    else:
                        go(cp)
        sent(attb.at[0:480, :], dsm, home)
        sent(attb, dsm, away)

    def exchange(g, cond):
        cols = pl.ds(*groups[g])
        send(rcopy(cotb.at[:, cols], coto.at[:, cols], es.at[g], er.at[g], core_p), cond)

    def arrived(g):
        @pl.when(m == 0)
        def _():
            for n, (pg, col, width, _) in enumerate(parts):
                if pg == g:
                    wait_on(cotb.at[:, pl.ds(col, width)], cr.at[n])

    def partials(g):
        cols = pl.ds(*groups[g])
        wait_on(coto.at[:, cols], er.at[g])
        for r in range(2):
            rows = pl.ds(r * 640, 640)
            gbuf[rows, cols] = dot(xts[c, rows, :], cotb[:, cols], ((1,), (0,))) + dot(
                xto[rows, :], coto[:, cols], ((1,), (0,))
            )

    def dest(o):
        return pl.multiple_of(lax.rem(z + nz + o, nz) * 160, 16)

    def span_of(d, k):
        return pl.ds(80 * d, 80) if k == 0 else pl.ds(0, 160)

    def ring(g, k):
        cols = pl.ds(*groups[g])
        for d in range(2):
            o = (4 - k) if d == 0 else (k - 4)
            first = dest(o)
            own, rest = pl.ds(80 * d, 80), pl.ds(80 - 80 * d, 80)
            mine = gbuf[pl.ds(first + 80 * d, 80), cols]
            if k >= 1:
                wait_on(rbuf.at[d, k - 1, span_of(d, k - 1), cols], rr.at[d, g, k - 1])
            if k == 0:
                sbuf[d, k, own, cols] = mine.astype(BF16)
            elif k == 1:
                sbuf[d, k, own, cols] = (mine + rbuf[d, 0, own, cols].astype(F32)).astype(BF16)
                sbuf[d, k, rest, cols] = gbuf[pl.ds(first + 80 - 80 * d, 80), cols].astype(BF16)
            else:
                sbuf[d, k, :, cols] = (
                    gbuf[pl.ds(first, 160), cols] + rbuf[d, k - 1, :, cols].astype(F32)
                ).astype(BF16)
            piece = sbuf.at[d, k, span_of(d, k), cols]
            cp = rcopy(
                piece, rbuf.at[d, k, span_of(d, k), cols],
                rs.at[d, g, min(k, 1)], rr.at[d, g, k], up_z if d == 0 else dn_z,
            )
            if k == 0:
                send(cp)
            else:
                go(cp)
        if k == 3:
            for d in range(2):
                sent(sbuf.at[d, 1:4, :, cols], rs.at[d, g, 1])

    def finish(g):
        cols = pl.ds(*groups[g])
        for d in range(2):
            wait_on(rbuf.at[d, 3, :, cols], rr.at[d, g, 3])
        fbuf[:, cols] = (
            gbuf[pl.ds(dest(0), 160), cols]
            + (rbuf[0, 3, :, cols].astype(F32) + rbuf[1, 3, :, cols].astype(F32))
        ).astype(BF16)

    def deliver(g):
        for n, (pg, col, width, outer) in enumerate(parts):
            if pg != g:
                continue
            piece = fbuf.at[:, pl.ds(col, width)]
            dst = obuf.at[:, pl.ds(col, width)]
            straight = (m == 1) if outer else (m <= 1)
            send(rcopy(piece, dst, fs.at[n, 0], fr.at[n], turn), jnp.logical_and(straight, away))

            @pl.when(jnp.logical_and(straight, home))
            def _():
                pltpu.make_async_copy(piece, dst, fr.at[n]).start()

            if outer:
                send(rcopy(piece, dst, fs.at[n, 1], fr.at[n], at(c=1 - yh, yh=c)), m == 0)

    def received(g):
        for n, (pg, col, width, _) in enumerate(parts):
            if pg == g:
                wait_on(obuf.at[:, pl.ds(col, width)], fr.at[n])
                for k in range(width // 128):
                    p = col // 128 + k
                    grad_ref[p % 3, :, pl.ds(p // 3 * 128, 128)] = obuf[:, pl.ds(p * 128, 128)]

    def direction():
        for dm in range(2):
            for dx in range(4):
                for b in range(2):
                    wait_on(
                        dbuf.at[lax.rem(m + dm, 2), :, pl.ds(pl.multiple_of((lax.rem(x + nx - dx, nx) * 2 + b) * 384, 128), 384)],
                        dr.at[dm, dx, b],
                    )
        dir_ref[...] = (dbuf[1].astype(F32) - dbuf[0].astype(F32)).astype(BF16)

    def shared(g):
        arrived(g)
        exchange(g, m == 0)

    def launch(h):
        attend(h)
        key_side(h, 2)
        if h == 2:
            spread(3)
            exchange(3, fake)
        key_side(h, 1)
        spread(h)
        exchange(h, fake)

    noise(0)
    x_own(0)
    w_event(0, 0, 0, home)
    w_event(0, 0, 1, home)
    w_event(1, 0, 0, home)
    w_event(1, 0, 1, home)
    noise(1)
    x_own(1)
    w_event(0, 0, 0, away)
    w_event(0, 0, 1, away)
    w_turn(1)
    stage(0, 1, 0)
    x_y(0)
    w_event(2, 0, 0, home)
    noise(2)
    x_own(2)
    stage(0, 1, 1)
    w_event(2, 0, 1, home)
    x_y(1)
    stage(0, 2, 0)
    w_turn(2)
    w_event(1, 0, 0, away)
    x_z(0)
    noise(3)
    x_own(3)
    stage(0, 2, 1)
    w_event(1, 0, 1, away)
    x_y(2)
    stage(0, 3, 0)
    x_z(1)
    stage(0, 3, 1)
    side_inputs()
    x_ready(0)
    turned(0)
    last(0)
    stage(1, 1, 0)
    x_y(3)
    x_z(2)
    multiply_columns(0)
    turned_send(0)
    stage(1, 1, 1)
    x_z(3)
    x_ready(1)
    multiply_columns(1)
    turned(1)
    stage(1, 2, 0)
    w_event(2, 0, 0, away)
    x_ready(2)
    multiply_columns(2)
    turned(2)
    turned_send(1)
    stage(1, 2, 1)
    w_event(2, 0, 1, away)
    x_ready(3)
    multiply_columns(3)
    keep(0)
    stage(1, 3, 0)
    multiply(1, 0, 1)
    stage(1, 3, 1)
    attention_inputs()
    launch(0)
    turned(3)
    turned_send(2)
    turned_send(3)
    last(1)
    multiply(1, 2, 3, 4)
    stage(2, 1, 0)
    multiply(1, 5, 6, 7)
    keep(1)
    stage(2, 1, 1)
    launch(1)
    stage(2, 2, 0)
    multiply(2, 0)
    for q in range(2):
        wait_on(xto.at[pl.ds(q * 640, 640), :], xtr.at[q])
    shared(0)
    stage(2, 2, 1)
    multiply(2, 1, 2)
    partials(0)
    stage(2, 3, 0)
    multiply(2, 3, 4)
    stage(2, 3, 1)
    ring(0, 0)
    shared(1)
    partials(1)
    ring(1, 0)
    early = len(pending)
    last(2)
    multiply(2, 5, 6, 7)
    keep(2)
    launch(2)
    ring(0, 1)
    ring(1, 1)
    direction_send()
    ring(0, 2)
    ring(1, 2)
    settle(early)
    shared(3)
    ring(0, 3)
    partials(3)
    ring(3, 0)
    shared(2)
    ring(1, 3)
    partials(2)
    ring(2, 0)
    finish(0)
    deliver(0)
    ring(3, 1)
    ring(2, 1)
    finish(1)
    deliver(1)
    ring(3, 2)
    ring(2, 2)
    direction()
    ring(3, 3)
    ring(2, 3)
    received(0)
    finish(3)
    deliver(3)
    finish(2)
    deliver(2)
    received(1)
    received(3)
    received(2)
    settle(len(pending))


def per_device(latents, noise, noise_level, group_index, projections, upstream):
    weights = jnp.transpose(projections[0], (1, 0, 2))
    groups = group_index
    dma = pltpu.SemaphoreType.DMA
    vmem = pltpu.VMEM
    anywhere = pl.BlockSpec(memory_space=pl.ANY)
    direction, grads = pl.pallas_call(
        step_kernel,
        out_shape=(
            jax.ShapeDtypeStruct((32, 3072), BF16),
            jax.ShapeDtypeStruct((3, 160, 384), BF16),
        ),
        in_specs=[anywhere, anywhere, pl.BlockSpec(memory_space=pltpu.SMEM), anywhere, anywhere, anywhere],
        out_specs=(pl.BlockSpec(memory_space=pltpu.VMEM), pl.BlockSpec(memory_space=pltpu.VMEM)),
        scratch_shapes=[
            vmem((3, 5120, 384), BF16),
            vmem((4, 512, 1280), BF16),
            vmem((4, 256, 1280), BF16),
            vmem((4, 256, 1280), BF16),
            vmem((512, 384), F32),
            vmem((3, 512, 384), BF16),
            vmem((512, 384), BF16),
            vmem((1, 512), jnp.int32),
            vmem((512, 128), jnp.int32),
            vmem((512, 384), BF16),
            vmem((512, 1152), BF16),
            vmem((512, 1152), BF16),
            vmem((2, 1280, 512), BF16),
            vmem((1280, 512), BF16),
            vmem((512, 512), BF16),
            vmem((512, 512), BF16),
            vmem((1280, 1152), F32),
            vmem((2, 4, 160, 1152), BF16),
            vmem((2, 4, 160, 1152), BF16),
            vmem((160, 1152), BF16),
            vmem((160, 1152), BF16),
            vmem((2, 32, 3072), BF16),
            dma((3, 8, 2)), dma((3, 8)), dma((3,)), dma((3,)), dma((3,)),
            dma((4, 2)), dma((4, 2)), dma((4,)), dma((4,)),
            dma((4, 2)), dma((4,)), dma((2,)), dma((2,)),
            dma((6,)), dma((6,)), dma((4,)), dma((4,)),
            dma((2, 4, 4)), dma((2, 4, 2)), dma((6,)), dma((6, 2)),
            dma((2, 4, 2)), dma,
        ],
        compiler_params=pltpu.CompilerParams(
            collective_id=0, has_side_effects=True, vmem_limit_bytes=62 << 20
        ),
    )(latents[0], noise[0], noise_level, weights, upstream[0], groups)
    grads = jnp.transpose(grads.astype(F32), (1, 0, 2))
    return direction[None], grads


def solution(mesh):
    split = Mesh(
        mesh.devices.reshape(2, mesh.shape["seq"] // 2, 2, mesh.shape["fsdp"] // 2, 2), AXES
    )
    clip, heads = ("z", "yh"), ("x", "c")
    return jax.shard_map(
        per_device,
        mesh=split,
        in_specs=(
            P(clip, "m", None),
            P(clip, "m", None),
            P(clip),
            P(clip, None),
            P("m", clip, None, heads),
            P(clip, None, heads),
        ),
        out_specs=(P(clip, ("m", "x", "c"), None), P(("m", "z", "yh"), None, heads)),
        check_vma=False,
    )
```

```python
import math

import jax
import jax.numpy as jnp
from jax import lax
from jax.experimental import pallas as pl
from jax.experimental.pallas import tpu as pltpu
from jax.sharding import Mesh
from jax.sharding import PartitionSpec as P

HEAD = 128
AXES = ("m", "x", "c", "z", "yh")
MESH_ID = pl.DeviceIdType.MESH
F32 = jnp.float32
BF16 = jnp.bfloat16
OFFSETS = (0, -1, 1, -2, 2, -3, 3, 4)


def dot(a, b, dims):
    return lax.dot_general(a, b, (dims, ((), ())), preferred_element_type=F32)


def step_kernel(
    lat_ref, noi_ref, lvl_ref, proj_ref, up_ref, gi_ref,
    dir_ref, grad_ref,
    wbuf, own, xbuf, latv, noiv, acc, tri, upb, gib, gcol, attb, cotb, coto,
    xts, xto, pbuf, dsbuf, gbuf, sbuf, rbuf, fbuf, obuf, dbuf,
    wr, wc, ws, wcs, wos, wl, ya, xa, xs, xxs, lsem, usem, xtr, xtss, cr, cs, er, es,
    rr, rs, fr, fs, dr, dsm,
):
    m, x, c, z, yh = (lax.axis_index(a) for a in AXES)
    nz = lax.axis_size("z")
    nx = lax.axis_size("x")
    home = c == yh
    away = c != yh

    def at(**k):
        return k

    core_p = at(c=1 - c)
    sib = at(m=1 - m)
    out = at(m=1 - m, yh=1 - yh)
    turn = at(c=yh, yh=c)
    up_z = at(z=lax.rem(z + 1, nz))
    dn_z = at(z=lax.rem(z + nz - 1, nz))
    blk = [lax.rem(z + nz + o, nz) for o in OFFSETS]

    def rcopy(src, dst, ss, rsem, dev):
        return pltpu.make_async_remote_copy(
            src_ref=src, dst_ref=dst, send_sem=ss, recv_sem=rsem,
            device_id=dev, device_id_type=MESH_ID,
        )

    def wait_on(ref, sem):
        pltpu.make_async_copy(ref, ref, sem).wait()

    pending = []

    def go(cp, cond=None):
        if cond is None:
            cp.start()
        else:
            pl.when(cond)(cp.start)

    def send(cp, cond=None):
        go(cp, cond)
        pending.append((cp.wait_send, cond))

    def sent(ref, sem, cond=None):
        pending.append((lambda: wait_on(ref, sem), cond))

    def only(cond, *calls):
        @pl.when(cond)
        def _():
            for call, *arguments in calls:
                call(*arguments)

    def settle(number):
        for wait, cond in pending[:number]:
            if cond is None:
                wait()
            else:
                pl.when(cond)(wait)
        del pending[:number]

    rows_m = pl.ds(pl.multiple_of(m * 256, 256), 256)

    def read(p, which):
        src, dst = ((lat_ref, latv), (noi_ref, noiv))[which]
        return pltpu.make_async_copy(src.at[:, pl.ds(p * 1280, 1280)], dst.at[p], lsem.at[p, which])

    def w_rows(zb, core, i):
        return pl.ds(pl.multiple_of(zb * 640 + core * 320 + i * 160, 16), 160)

    def own_chunk(h, i):
        return wbuf.at[h, w_rows(z, yh, i), :]

    def stage_own(h, i, dst, sem):
        for j in range(3):
            pltpu.make_async_copy(
                proj_ref.at[j, pl.ds(160 * i, 160), pl.ds(128 * h, 128)],
                dst.at[:, pl.ds(128 * j, 128)], sem,
            ).start()

    @pl.when(home)
    def _():
        for h in range(3):
            for i in range(2):
                stage_own(h, i, own_chunk(h, i), wr.at[h, 0, i])
            if h < 2:
                for p in (2 * h, 2 * h + 1):
                    read(p, 0).start()
                    read(p, 1).start()

    @pl.when(away)
    def _():
        for h in range(3):
            for i in range(2):
                stage_own(h, i, own.at[h, i], wl.at[h, i])

    barrier = pltpu.get_barrier_semaphore()
    count = 0
    for dm in range(2):
        for dx in range(4):
            for dc in range(2):
                for dy in range(2):
                    if dm + dx + dc + dy == 0:
                        continue
                    peer = at(
                        m=lax.rem(m + dm, 2), x=lax.rem(x + dx, nx),
                        c=lax.rem(c + dc, 2), yh=lax.rem(yh + dy, 2),
                    )
                    pl.semaphore_signal(barrier, inc=1, device_id=peer, device_id_type=MESH_ID)
                    count += 1
    for peer in (up_z, dn_z):
        pl.semaphore_signal(barrier, inc=1, device_id=peer, device_id_type=MESH_ID)
        count += 1
    pl.semaphore_wait(barrier, count)

    def w_turn(h):
        for i in range(2):
            pl.when(away)(lambda: wait_on(own.at[h, i], wl.at[h, i]))
            go(rcopy(own.at[h, i], own_chunk(h, i), wos.at[h], wr.at[h, 0, i], turn), away)
        sent(wbuf.at[h, 0:320, :], wos.at[h], away)

    w_turn(0)

    def side_inputs():
        send(rcopy(gi_ref, gib, usem.at[2], usem.at[3], turn), away)
        send(rcopy(up_ref, upb, usem.at[0], usem.at[1], turn), jnp.logical_and(away, m == 1))

        @pl.when(jnp.logical_or(home, m == 0))
        def _():
            pltpu.make_async_copy(up_ref, upb, usem.at[1]).start()

        @pl.when(home)
        def _():
            pltpu.make_async_copy(gi_ref, gib, usem.at[3]).start()

    rate = lvl_ref[0]

    up_x = at(x=lax.rem(x + 1, nx))
    dn_x = at(x=lax.rem(x + nx - 1, nx))

    def quarter(half, step):
        first = half * 256 + lax.rem(x + nx + step, nx) * 64
        return pl.ds(pl.multiple_of(first, 64), 64)

    def noise(p):
        @pl.when(home)
        def _():
            read(p, 0).wait()
            read(p, 1).wait()
            for lo in (0, 640):
                xbuf[p, rows_m, lo : lo + 640] = (
                    (1.0 - rate) * latv[p, :, lo : lo + 640].astype(F32)
                    + rate * noiv[p, :, lo : lo + 640].astype(F32)
                ).astype(BF16)

    def x_own(p):
        for q in range(2):
            piece = xbuf.at[p, quarter(m, q), :]
            go(rcopy(piece, piece, xs.at[p], ya.at[p, 0], sib), home)
            go(rcopy(piece, piece, xs.at[p], ya.at[p, 0], out), home)

    def x_side(p, kind, q, cond):
        piece = xbuf.at[p, quarter((1 - m) if kind == 0 else m, q), :]
        go(rcopy(piece, piece, xxs.at[p], xa.at[p, kind], up_x if q == 0 else dn_x), cond)

    def x_y(p):
        wait_on(xbuf.at[p, 0:128, :], ya.at[p, 0])
        for q in range(2):
            piece = xbuf.at[p, quarter(1 - m, q), :]
            if p % 2 == 1:
                go(rcopy(piece, piece, xs.at[p], ya.at[p, 1], out), home)
            else:
                go(rcopy(piece, piece, xs.at[p], ya.at[p, 1], sib), away)
            x_side(p, 0, q, None)

    def x_z(p):
        @pl.when(away)
        def _():
            wait_on(xbuf.at[p, 0:128, :], ya.at[p, 1])

        for q in range(2):
            x_side(p, 1, q, away)

    def x_ready(p):
        wait_on(xbuf.at[p, 0:128, :], xa.at[p, 0])

        @pl.when(away)
        def _():
            wait_on(xbuf.at[p, 0:128, :], xa.at[p, 1])

        sent(xbuf.at[p, 0 : 256 + 128 * (p % 2), :], xs.at[p], home)
        if p % 2 == 0:
            sent(xbuf.at[p, 0:128, :], xs.at[p], away)
        sent(xbuf.at[p, 0:128, :], xxs.at[p], home)
        sent(xbuf.at[p, 0:256, :], xxs.at[p], away)

    def w_event(h, k, i, cond=None):
        piece = wbuf.at[h, w_rows(blk[k], c, i), :]
        if cond is None:
            wait_on(piece, wr.at[h, k, i])
        else:
            pl.when(cond)(lambda: wait_on(piece, wr.at[h, k, i]))
        o = OFFSETS[k]
        if -3 < o <= 0 or (o == -3 and i == 0):
            to = OFFSETS.index(o - 1 if o > -3 else 4)
            go(rcopy(piece, piece, ws.at[h], wr.at[h, to, i], up_z), cond)
        if 0 <= o < 3 or (o == 3 and i == 1):
            go(rcopy(piece, piece, ws.at[h], wr.at[h, OFFSETS.index(o + 1), i], dn_z), cond)
        go(rcopy(piece, piece, wcs.at[h], wc.at[h, k], core_p), cond)

    def stage(h, n, i):
        w_event(h, 2 * n - 1, i)
        w_event(h, 2 * n, i)

    def last(h):
        w_event(h, 7, 0)
        w_event(h, 7, 1)
        sent(wbuf.at[h, 0:2240, :], ws.at[h])
        sent(wbuf.at[h, 0:2560, :], wcs.at[h])

    def w_other(h, k):
        first = pl.multiple_of(blk[k] * 640 + (1 - c) * 320, 64)
        wait_on(wbuf.at[h, pl.ds(first, 320), :], wc.at[h, k])

    def gather(first, part):
        if first:
            acc[...] = part
        else:
            acc[...] += part

    def multiply_columns(p):
        if p == 0:
            for k in range(8):
                w_other(0, k)
        gather(p == 0, dot(xbuf[p], wbuf[0, p * 1280 : (p + 1) * 1280, :], ((1,), (0,))))

    def multiply(h, *blocks):
        for k in blocks:
            w_other(h, k)
            cols = pl.ds(pl.multiple_of(lax.rem(blk[k], 2) * 640, 128), 640)
            rows = pl.ds(pl.multiple_of(blk[k] * 640, 128), 640)
            gather(k == 0, dot(xbuf[blk[k] // 2, :, cols], wbuf[h, rows, :], ((1,), (0,))))

    def keep(h):
        tri[h] = acc[...].astype(BF16)

    def turned(p):
        @pl.when(m == p // 2)
        def _():
            base = (p % 2) * 640
            for i in range(10):
                t = xbuf[p, :, i * 128 : (i + 1) * 128].T
                r = i * 128
                while r < (i + 1) * 128:
                    end = min((i + 1) * 128, (r // 160 + 1) * 160)
                    first = base + (r // 320) * 160 + r % 160
                    xts[(r % 320) // 160, pl.ds(first, end - r), :] = t[r - i * 128 : end - i * 128, :]
                    r = end

    def turned_send(p):
        span = pl.ds((p % 2) * 640, 640)
        send(
            rcopy(xts.at[1 - c, span, :], xto.at[span, :], xtss.at[p % 2], xtr.at[p % 2], core_p),
            m == p // 2,
        )

    def attention_inputs():
        wait_on(gib, usem.at[3])
        wait_on(upb, usem.at[1])
        gcol[...] = jnp.transpose(jnp.broadcast_to(gib[...], (128, 512)))

    scale = 1.0 / math.sqrt(HEAD)
    fake = m == 1
    def attend(h, *blocks):
        qc, kc, vc = (pl.ds(j * 128, 128) for j in range(3))
        hc = pl.ds(h * 128, 128)
        for b in blocks:
            nk = min(512, (b + 2) * 128)
            rows = pl.ds(b * 128, 128)
            s = dot(tri[h, rows, qc], tri[h, 0:nk, kc], ((1,), (1,))) * scale
            mine = gcol[rows, :]
            visible = gib[0:1, 0:nk] <= jnp.concatenate([mine] * (nk // 128), axis=1)
            s = jnp.where(visible, s, F32(-1e30))
            w = jnp.exp(s - jnp.max(s, axis=-1, keepdims=True))
            p = w * (1.0 / jnp.sum(w, axis=-1, keepdims=True))
            low = p.astype(BF16)
            attb[rows, hc] = dot(low, tri[h, 0:nk, vc], ((1,), (0,))).astype(BF16)

            @pl.when(fake)
            def _():
                dp = dot(upb[rows, hc], tri[h, 0:nk, vc], ((1,), (1,)))
                inner = jnp.sum(p * dp, axis=-1, keepdims=True)
                ds = (p * (dp - inner) * scale).astype(BF16)
                cotb[h * 3, rows, :] = dot(ds, tri[h, 0:nk, kc], ((1,), (0,))).astype(BF16)
                pbuf[rows, 0:nk] = low
                dsbuf[rows, 0:nk] = ds

    def key_side(h, j):
        left, right = (
            (dsbuf, tri.at[h, :, pl.ds(0, 128)]) if j == 1 else (pbuf, upb.at[:, pl.ds(h * 128, 128)])
        )

        @pl.when(fake)
        def _():
            for b in range(4):
                first = max(0, (b - 1) * 128)
                rows = pl.ds(first, 512 - first)
                keys = pl.ds(b * 128, 128)
                cotb[h * 3 + j, keys, :] = dot(
                    left[rows, keys], right[rows, :], ((0,), (0,))
                ).astype(BF16)

    parts = (
        (0, 0, 2, False), (0, 2, 1, True),
        (1, 3, 1, False), (1, 4, 2, True),
        (2, 6, 2, False),
        (3, 8, 1, True),
    )
    groups = ((0, 3), (3, 3), (6, 2), (8, 1))

    def blocks_of(g):
        return range(groups[g][0], groups[g][0] + groups[g][1])

    def side_by_side(ref, g):
        return jnp.concatenate([ref[p] for p in blocks_of(g)], axis=1)

    def spread(g):
        for n, (pg, first, number, outer) in enumerate(parts):
            if pg == g:
                piece = cotb.at[pl.ds(first, number)]
                send(rcopy(piece, piece, cs.at[n], cr.at[n], out if outer else sib), fake)

    def direction_send():
        for dm in range(2):
            for dx in range(4):
                for dc in range(2):
                    tm, tx, tc = lax.rem(m + dm, 2), lax.rem(x + dx, nx), lax.rem(c + dc, 2)
                    src = attb.at[pl.ds(pl.multiple_of((tm * 8 + tx * 2 + tc) * 32, 32), 32), :]
                    dst = dbuf.at[m, x * 2 + yh]
                    sem = dr.at[dm, dx, yh]
                    cp = rcopy(src, dst, dsm, sem, at(m=tm, x=tx, c=tc, yh=c))
                    if dm + dx + dc == 0:
                        go(cp, away)

                        @pl.when(home)
                        def _():
                            pltpu.make_async_copy(src, dst, sem).start()
                    else:
                        go(cp)
        sent(attb.at[0:480, :], dsm, home)
        sent(attb, dsm, away)

    def exchange(g, cond):
        span = pl.ds(*groups[g])
        send(rcopy(cotb.at[span], coto.at[span], es.at[g], er.at[g], core_p), cond)

    def arrived(g):
        @pl.when(m == 0)
        def _():
            for n, (pg, first, number, _) in enumerate(parts):
                if pg == g:
                    wait_on(cotb.at[pl.ds(first, number)], cr.at[n])

    def partials(g):
        wait_on(coto.at[pl.ds(*groups[g])], er.at[g])
        mine, other = side_by_side(cotb, g), side_by_side(coto, g)
        for r in range(2):
            rows = pl.ds(r * 640, 640)
            both = dot(xts[c, rows, :], mine, ((1,), (0,))) + dot(xto[rows, :], other, ((1,), (0,)))
            for n, p in enumerate(blocks_of(g)):
                gbuf[p, rows, :] = both[:, n * 128 : (n + 1) * 128]

    def dest(o):
        return pl.multiple_of(lax.rem(z + nz + o, nz) * 160, 16)

    def span_of(d, k):
        return pl.ds(80 * d, 80) if k == 0 else pl.ds(0, 160)

    def ring(g, k):
        span = pl.ds(*groups[g])
        for d in range(2):
            o = (4 - k) if d == 0 else (k - 4)
            first = dest(o)
            mine, rest = pl.ds(80 * d, 80), pl.ds(80 - 80 * d, 80)
            if k >= 1:
                wait_on(rbuf.at[d, k - 1, span, span_of(d, k - 1), :], rr.at[d, g, k - 1])
            for p in blocks_of(g):
                if k == 0:
                    sbuf[d, k, p, mine, :] = gbuf[p, pl.ds(first + 80 * d, 80), :].astype(BF16)
                elif k == 1:
                    sbuf[d, k, p, mine, :] = (
                        gbuf[p, pl.ds(first + 80 * d, 80), :] + rbuf[d, 0, p, mine, :].astype(F32)
                    ).astype(BF16)
                    sbuf[d, k, p, rest, :] = gbuf[p, pl.ds(first + 80 - 80 * d, 80), :].astype(BF16)
                else:
                    sbuf[d, k, p, :, :] = (
                        gbuf[p, pl.ds(first, 160), :] + rbuf[d, k - 1, p, :, :].astype(F32)
                    ).astype(BF16)
            go(rcopy(
                sbuf.at[d, k, span, span_of(d, k), :], rbuf.at[d, k, span, span_of(d, k), :],
                rs.at[d, g, min(k, 1)], rr.at[d, g, k], up_z if d == 0 else dn_z,
            ))

    def ring_sent(g):
        span = pl.ds(*groups[g])
        for d in range(2):
            wait_on(sbuf.at[d, 0, span, span_of(d, 0), :], rs.at[d, g, 0])
            wait_on(sbuf.at[d, 1:4, span, :, :], rs.at[d, g, 1])

    def finish(g):
        for d in range(2):
            wait_on(rbuf.at[d, 3, pl.ds(*groups[g]), :, :], rr.at[d, g, 3])
        for p in blocks_of(g):
            fbuf[p] = (
                gbuf[p, pl.ds(dest(0), 160), :]
                + (rbuf[0, 3, p].astype(F32) + rbuf[1, 3, p].astype(F32))
            ).astype(BF16)

    def deliver(g):
        for n, (pg, first, number, outer) in enumerate(parts):
            if pg != g:
                continue
            piece = fbuf.at[pl.ds(first, number)]
            dst = obuf.at[pl.ds(first, number)]
            straight = (m == 1) if outer else (m <= 1)
            send(rcopy(piece, dst, fs.at[n, 0], fr.at[n], turn), jnp.logical_and(straight, away))

            @pl.when(jnp.logical_and(straight, home))
            def _():
                pltpu.make_async_copy(piece, dst, fr.at[n]).start()

            if outer:
                send(rcopy(piece, dst, fs.at[n, 1], fr.at[n], at(c=1 - yh, yh=c)), m == 0)

    def received(g):
        for n, (pg, first, number, _) in enumerate(parts):
            if pg == g:
                wait_on(obuf.at[pl.ds(first, number)], fr.at[n])
                for p in range(first, first + number):
                    grad_ref[p % 3, :, pl.ds(p // 3 * 128, 128)] = obuf[p]

    def direction():
        for dm in range(2):
            for dx in range(4):
                for b in range(2):
                    wait_on(dbuf.at[lax.rem(m + dm, 2), lax.rem(x + nx - dx, nx) * 2 + b], dr.at[dm, dx, b])
        for n in range(8):
            dir_ref[:, pl.ds(n * 384, 384)] = (dbuf[1, n].astype(F32) - dbuf[0, n].astype(F32)).astype(BF16)

    def shared(g):
        arrived(g)
        exchange(g, m == 0)

    def values_done(h):
        key_side(h, 2)
        if h == 2:
            spread(3)
            exchange(3, fake)

    def keys_done(h):
        key_side(h, 1)
        spread(h)
        exchange(h, fake)

    w_event(0, 0, 0, home)
    w_event(0, 0, 1, home)
    noise(0)
    x_own(0)
    noise(1)
    w_event(0, 0, 0, away)
    w_event(0, 0, 1, away)
    w_turn(1)
    stage(0, 1, 0)
    w_event(1, 0, 0, home)
    w_event(1, 0, 1, home)
    x_own(1)
    x_y(0)
    noise(2)
    stage(0, 1, 1)
    w_event(2, 0, 0, home)
    w_event(2, 0, 1, home)
    w_turn(2)
    x_own(2)
    x_y(1)
    stage(0, 2, 0)
    w_event(1, 0, 0, away)
    noise(3)
    x_own(3)
    x_z(0)
    stage(0, 2, 1)
    w_event(1, 0, 1, away)
    x_y(2)
    stage(0, 3, 0)
    x_z(1)
    stage(0, 3, 1)
    x_ready(0)
    turned(0)
    last(0)
    stage(1, 1, 0)
    x_y(3)
    x_z(2)
    stage(1, 1, 1)
    side_inputs()
    x_ready(1)
    turned(1)
    turned_send(0)
    stage(1, 2, 0)
    w_event(2, 0, 0, away)
    multiply_columns(0)
    multiply_columns(1)
    stage(1, 2, 1)
    w_event(2, 0, 1, away)
    x_z(3)
    x_ready(2)
    multiply_columns(2)
    turned(2)
    turned_send(1)
    stage(1, 3, 0)
    x_ready(3)
    multiply_columns(3)
    keep(0)
    stage(1, 3, 1)
    stage(2, 1, 0)
    attention_inputs()
    attend(0, 0, 1)
    multiply(1, 0, 1, 2)
    last(1)
    attend(0, 2, 3)
    values_done(0)
    keys_done(0)
    stage(2, 1, 1)
    multiply(1, 3, 4, 5, 6, 7)
    keep(1)
    stage(2, 2, 0)
    attend(1, 0, 1)
    stage(2, 2, 1)
    attend(1, 2, 3)
    values_done(1)
    keys_done(1)
    stage(2, 3, 0)
    turned(3)
    turned_send(2)
    turned_send(3)
    multiply(2, 0, 1, 2)
    stage(2, 3, 1)
    for q in range(2):
        wait_on(xto.at[pl.ds(q * 640, 640), :], xtr.at[q])
    shared(0)
    partials(0)
    ring(0, 0)
    multiply(2, 3, 4)
    teacher = m == 0
    only(fake, (partials, 1), (ring, 1, 0))
    early = len(pending)
    last(2)
    multiply(2, 5, 6, 7)
    keep(2)
    ring(0, 1)
    attend(2, 0, 1)
    only(fake, (ring, 1, 1))
    attend(2, 2, 3)
    values_done(2)
    keys_done(2)
    shared(1)
    only(teacher, (partials, 1), (ring, 1, 0))
    ring(0, 2)
    only(teacher, (ring, 1, 1))
    only(fake, (ring, 1, 2))
    ring(0, 3)
    direction_send()
    only(teacher, (ring, 1, 2))
    only(fake, (ring, 1, 3))
    settle(early)
    shared(3)
    partials(3)
    ring(3, 0)
    only(teacher, (ring, 1, 3))
    shared(2)
    partials(2)
    ring(2, 0)
    finish(0)
    deliver(0)
    ring(3, 1)
    ring(2, 1)
    finish(1)
    deliver(1)
    ring(3, 2)
    ring(2, 2)
    direction()
    ring(3, 3)
    ring(2, 3)
    received(0)
    finish(3)
    deliver(3)
    finish(2)
    deliver(2)
    received(1)
    received(3)
    for g in range(4):
        ring_sent(g)
    received(2)
    settle(len(pending))


def widen_kernel(direction_ref, grads_ref, direction_out, grads_out):
    direction_out[...] = direction_ref[...]
    grads_out[...] = grads_ref[...].astype(F32)


def per_device(latents, noise, noise_level, group_index, projections, upstream):
    weights = jnp.transpose(projections[0], (1, 0, 2))
    groups = group_index
    dma = pltpu.SemaphoreType.DMA
    vmem = pltpu.VMEM
    anywhere = pl.BlockSpec(memory_space=pl.ANY)
    direction, grads = pl.pallas_call(
        step_kernel,
        out_shape=(
            jax.ShapeDtypeStruct((32, 3072), BF16),
            jax.ShapeDtypeStruct((3, 160, 384), BF16),
        ),
        in_specs=[anywhere, anywhere, pl.BlockSpec(memory_space=pltpu.SMEM), anywhere, anywhere, anywhere],
        out_specs=(pl.BlockSpec(memory_space=pltpu.VMEM), pl.BlockSpec(memory_space=pltpu.VMEM)),
        scratch_shapes=[
            vmem((3, 5120, 384), BF16),
            vmem((3, 2, 160, 384), BF16),
            vmem((4, 512, 1280), BF16),
            vmem((4, 256, 1280), BF16),
            vmem((4, 256, 1280), BF16),
            vmem((512, 384), F32),
            vmem((3, 512, 384), BF16),
            vmem((512, 384), BF16),
            vmem((1, 512), jnp.int32),
            vmem((512, 128), jnp.int32),
            vmem((512, 384), BF16),
            vmem((9, 512, 128), BF16),
            vmem((9, 512, 128), BF16),
            vmem((2, 1280, 512), BF16),
            vmem((1280, 512), BF16),
            vmem((512, 512), BF16),
            vmem((512, 512), BF16),
            vmem((9, 1280, 128), F32),
            vmem((2, 4, 9, 160, 128), BF16),
            vmem((2, 4, 9, 160, 128), BF16),
            vmem((9, 160, 128), BF16),
            vmem((9, 160, 128), BF16),
            vmem((2, 8, 32, 384), BF16),
            dma((3, 8, 2)), dma((3, 8)), dma((3,)), dma((3,)), dma((3,)), dma((3, 2)),
            dma((4, 2)), dma((4, 2)), dma((4,)), dma((4,)),
            dma((4, 2)), dma((4,)), dma((2,)), dma((2,)),
            dma((6,)), dma((6,)), dma((4,)), dma((4,)),
            dma((2, 4, 4)), dma((2, 4, 2)), dma((6,)), dma((6, 2)),
            dma((2, 4, 2)), dma,
        ],
        compiler_params=pltpu.CompilerParams(
            collective_id=0, has_side_effects=True, vmem_limit_bytes=62 << 20
        ),
    )(latents[0], noise[0], noise_level, weights, upstream[0], groups)
    direction, grads = pl.pallas_call(
        widen_kernel,
        out_shape=(
            jax.ShapeDtypeStruct((32, 3072), BF16),
            jax.ShapeDtypeStruct((3, 160, 384), F32),
        ),
        in_specs=[pl.BlockSpec(memory_space=pltpu.VMEM)] * 2,
        out_specs=(pl.BlockSpec(memory_space=pltpu.VMEM), pl.BlockSpec(memory_space=pltpu.VMEM)),
    )(direction, grads)
    return direction[None], jnp.transpose(grads, (1, 0, 2))


def solution(mesh):
    split = Mesh(
        mesh.devices.reshape(2, mesh.shape["seq"] // 2, 2, mesh.shape["fsdp"] // 2, 2), AXES
    )
    clip, heads = ("z", "yh"), ("x", "c")
    return jax.shard_map(
        per_device,
        mesh=split,
        in_specs=(
            P(clip, "m", None),
            P(clip, "m", None),
            P(clip),
            P(clip, None),
            P("m", clip, None, heads),
            P(clip, None, heads),
        ),
        out_specs=(P(clip, ("m", "x", "c"), None), P(("m", "z", "yh"), None, heads)),
        check_vma=False,
    )
```

```python
import math

import jax
import jax.numpy as jnp
from jax import lax
from jax.experimental import pallas as pl
from jax.experimental.pallas import tpu as pltpu
from jax.sharding import Mesh
from jax.sharding import PartitionSpec as P

HEAD = 128
AXES = ("m", "x", "c", "z", "yh")
MESH_ID = pl.DeviceIdType.MESH
F32 = jnp.float32
BF16 = jnp.bfloat16
OFFSETS = (0, -1, 1, -2, 2, -3, 3, 4)


def dot(a, b, dims):
    return lax.dot_general(a, b, (dims, ((), ())), preferred_element_type=F32)


def step_kernel(
    lat_ref, noi_ref, lvl_ref, proj_ref, up_ref, gi_ref,
    dir_ref, grad_ref,
    wbuf, own, xbuf, latv, noiv, acc, tri, upb, gib, gcol, attb, cotb, coto,
    xts, xto, pbuf, dsbuf, gbuf, sbuf, rbuf, fbuf, obuf, dbuf,
    wr, wc, ws, wcs, wos, wl, ya, xa, xs, xxs, lsem, usem, xtr, xtss, cr, cs, er, es,
    rr, rs, fr, fs, dr, dsm,
):
    m, x, c, z, yh = (lax.axis_index(a) for a in AXES)
    nz = lax.axis_size("z")
    nx = lax.axis_size("x")
    home = c == yh
    away = c != yh

    def at(**k):
        return k

    core_p = at(c=1 - c)
    sib = at(m=1 - m)
    out = at(m=1 - m, yh=1 - yh)
    turn = at(c=yh, yh=c)
    up_z = at(z=lax.rem(z + 1, nz))
    dn_z = at(z=lax.rem(z + nz - 1, nz))
    blk = [lax.rem(z + nz + o, nz) for o in OFFSETS]

    def rcopy(src, dst, ss, rsem, dev):
        return pltpu.make_async_remote_copy(
            src_ref=src, dst_ref=dst, send_sem=ss, recv_sem=rsem,
            device_id=dev, device_id_type=MESH_ID,
        )

    def wait_on(ref, sem):
        pltpu.make_async_copy(ref, ref, sem).wait()

    pending = []

    def go(cp, cond=None):
        if cond is None:
            cp.start()
        else:
            pl.when(cond)(cp.start)

    def send(cp, cond=None):
        go(cp, cond)
        pending.append((cp.wait_send, cond))

    def sent(ref, sem, cond=None):
        pending.append((lambda: wait_on(ref, sem), cond))

    def only(cond, *calls):
        @pl.when(cond)
        def _():
            for call, *arguments in calls:
                call(*arguments)

    def settle(number):
        for wait, cond in pending[:number]:
            if cond is None:
                wait()
            else:
                pl.when(cond)(wait)
        del pending[:number]

    rows_m = pl.ds(pl.multiple_of(m * 256, 256), 256)

    def read(p, which):
        src, dst = ((lat_ref, latv), (noi_ref, noiv))[which]
        return pltpu.make_async_copy(src.at[:, pl.ds(p * 1280, 1280)], dst.at[p], lsem.at[p, which])

    def w_rows(zb, core, i):
        return pl.ds(pl.multiple_of(zb * 640 + core * 320 + i * 160, 16), 160)

    def own_chunk(h, i):
        return wbuf.at[h, w_rows(z, yh, i), :]

    def stage_own(h, i, dst, sem):
        for j in range(3):
            pltpu.make_async_copy(
                proj_ref.at[j, pl.ds(160 * i, 160), pl.ds(128 * h, 128)],
                dst.at[:, pl.ds(128 * j, 128)], sem,
            ).start()

    @pl.when(home)
    def _():
        for h in range(3):
            for i in range(2):
                stage_own(h, i, own_chunk(h, i), wr.at[h, 0, i])
            if h < 2:
                for p in (2 * h, 2 * h + 1):
                    read(p, 0).start()
                    read(p, 1).start()

    @pl.when(away)
    def _():
        for h in range(3):
            for i in range(2):
                stage_own(h, i, own.at[h, i], wl.at[h, i])

    barrier = pltpu.get_barrier_semaphore()
    count = 0
    for dm in range(2):
        for dx in range(4):
            for dc in range(2):
                for dy in range(2):
                    if dm + dx + dc + dy == 0:
                        continue
                    peer = at(
                        m=lax.rem(m + dm, 2), x=lax.rem(x + dx, nx),
                        c=lax.rem(c + dc, 2), yh=lax.rem(yh + dy, 2),
                    )
                    pl.semaphore_signal(barrier, inc=1, device_id=peer, device_id_type=MESH_ID)
                    count += 1
    for peer in (up_z, dn_z):
        pl.semaphore_signal(barrier, inc=1, device_id=peer, device_id_type=MESH_ID)
        count += 1
    pl.semaphore_wait(barrier, count)

    def w_turn(h):
        for i in range(2):
            pl.when(away)(lambda: wait_on(own.at[h, i], wl.at[h, i]))
            go(rcopy(own.at[h, i], own_chunk(h, i), wos.at[h], wr.at[h, 0, i], turn), away)
        sent(wbuf.at[h, 0:320, :], wos.at[h], away)

    w_turn(0)

    def side_inputs():
        send(rcopy(gi_ref, gib, usem.at[2], usem.at[3], turn), away)
        send(rcopy(up_ref, upb, usem.at[0], usem.at[1], turn), jnp.logical_and(away, m == 1))

        @pl.when(jnp.logical_or(home, m == 0))
        def _():
            pltpu.make_async_copy(up_ref, upb, usem.at[1]).start()

        @pl.when(home)
        def _():
            pltpu.make_async_copy(gi_ref, gib, usem.at[3]).start()

    rate = lvl_ref[0]

    up_x = at(x=lax.rem(x + 1, nx))
    dn_x = at(x=lax.rem(x + nx - 1, nx))

    def quarter(half, step):
        first = half * 256 + lax.rem(x + nx + step, nx) * 64
        return pl.ds(pl.multiple_of(first, 64), 64)

    def noise(p):
        @pl.when(home)
        def _():
            read(p, 0).wait()
            read(p, 1).wait()
            for lo in (0, 640):
                xbuf[p, rows_m, lo : lo + 640] = (
                    (1.0 - rate) * latv[p, :, lo : lo + 640].astype(F32)
                    + rate * noiv[p, :, lo : lo + 640].astype(F32)
                ).astype(BF16)

    def x_own(p):
        for q in range(2):
            piece = xbuf.at[p, quarter(m, q), :]
            go(rcopy(piece, piece, xs.at[p], ya.at[p, 0], sib), home)
            go(rcopy(piece, piece, xs.at[p], ya.at[p, 0], out), home)

    def x_side(p, kind, q, cond):
        piece = xbuf.at[p, quarter((1 - m) if kind == 0 else m, q), :]
        go(rcopy(piece, piece, xxs.at[p], xa.at[p, kind], up_x if q == 0 else dn_x), cond)

    def x_y(p):
        wait_on(xbuf.at[p, 0:128, :], ya.at[p, 0])
        for q in range(2):
            piece = xbuf.at[p, quarter(1 - m, q), :]
            if p % 2 == 1:
                go(rcopy(piece, piece, xs.at[p], ya.at[p, 1], out), home)
            else:
                go(rcopy(piece, piece, xs.at[p], ya.at[p, 1], sib), away)
            x_side(p, 0, q, None)

    def x_z(p):
        @pl.when(away)
        def _():
            wait_on(xbuf.at[p, 0:128, :], ya.at[p, 1])

        for q in range(2):
            x_side(p, 1, q, away)

    def x_ready(p):
        wait_on(xbuf.at[p, 0:128, :], xa.at[p, 0])

        @pl.when(away)
        def _():
            wait_on(xbuf.at[p, 0:128, :], xa.at[p, 1])

        sent(xbuf.at[p, 0 : 256 + 128 * (p % 2), :], xs.at[p], home)
        if p % 2 == 0:
            sent(xbuf.at[p, 0:128, :], xs.at[p], away)
        sent(xbuf.at[p, 0:128, :], xxs.at[p], home)
        sent(xbuf.at[p, 0:256, :], xxs.at[p], away)

    def w_event(h, k, i, cond=None):
        piece = wbuf.at[h, w_rows(blk[k], c, i), :]
        if cond is None:
            wait_on(piece, wr.at[h, k, i])
        else:
            pl.when(cond)(lambda: wait_on(piece, wr.at[h, k, i]))
        o = OFFSETS[k]
        if -3 < o <= 0 or (o == -3 and i == 0):
            to = OFFSETS.index(o - 1 if o > -3 else 4)
            go(rcopy(piece, piece, ws.at[h], wr.at[h, to, i], up_z), cond)
        if 0 <= o < 3 or (o == 3 and i == 1):
            go(rcopy(piece, piece, ws.at[h], wr.at[h, OFFSETS.index(o + 1), i], dn_z), cond)
        go(rcopy(piece, piece, wcs.at[h], wc.at[h, k], core_p), cond)

    def stage(h, n, i):
        w_event(h, 2 * n - 1, i)
        w_event(h, 2 * n, i)

    def last(h):
        w_event(h, 7, 0)
        w_event(h, 7, 1)
        sent(wbuf.at[h, 0:2240, :], ws.at[h])
        sent(wbuf.at[h, 0:2560, :], wcs.at[h])

    def w_other(h, k):
        first = pl.multiple_of(blk[k] * 640 + (1 - c) * 320, 64)
        wait_on(wbuf.at[h, pl.ds(first, 320), :], wc.at[h, k])

    def gather(first, part):
        if first:
            acc[...] = part
        else:
            acc[...] += part

    def multiply_columns(p):
        if p == 0:
            for k in range(8):
                w_other(0, k)
        gather(p == 0, dot(xbuf[p], wbuf[0, p * 1280 : (p + 1) * 1280, :], ((1,), (0,))))

    def multiply(h, *blocks):
        for k in blocks:
            w_other(h, k)
            cols = pl.ds(pl.multiple_of(lax.rem(blk[k], 2) * 640, 128), 640)
            rows = pl.ds(pl.multiple_of(blk[k] * 640, 128), 640)
            gather(k == 0, dot(xbuf[blk[k] // 2, :, cols], wbuf[h, rows, :], ((1,), (0,))))

    def keep(h):
        tri[h] = acc[...].astype(BF16)

    def turned(p):
        @pl.when(m == p // 2)
        def _():
            base = (p % 2) * 640
            for i in range(10):
                t = xbuf[p, :, i * 128 : (i + 1) * 128].T
                r = i * 128
                while r < (i + 1) * 128:
                    end = min((i + 1) * 128, (r // 160 + 1) * 160)
                    first = base + (r // 320) * 160 + r % 160
                    xts[(r % 320) // 160, pl.ds(first, end - r), :] = t[r - i * 128 : end - i * 128, :]
                    r = end

    def turned_send(p):
        span = pl.ds((p % 2) * 640, 640)
        send(
            rcopy(xts.at[1 - c, span, :], xto.at[span, :], xtss.at[p % 2], xtr.at[p % 2], core_p),
            m == p // 2,
        )

    def attention_inputs():
        wait_on(gib, usem.at[3])
        wait_on(upb, usem.at[1])
        gcol[...] = jnp.transpose(jnp.broadcast_to(gib[...], (128, 512)))

    scale = 1.0 / math.sqrt(HEAD)
    fake = m == 1
    def attention(h, blocks, backward):
        qc, kc, vc = (pl.ds(j * 128, 128) for j in range(3))
        hc = pl.ds(h * 128, 128)
        for b in blocks:
            nk = min(512, (b + 2) * 128)
            rows = pl.ds(b * 128, 128)
            s = dot(tri[h, rows, qc], tri[h, 0:nk, kc], ((1,), (1,))) * scale
            mine = gcol[rows, :]
            visible = gib[0:1, 0:nk] <= jnp.concatenate([mine] * (nk // 128), axis=1)
            s = jnp.where(visible, s, F32(-1e30))
            w = jnp.exp(s - jnp.max(s, axis=-1, keepdims=True))
            p = w * (1.0 / jnp.sum(w, axis=-1, keepdims=True))
            low = p.astype(BF16)
            attb[rows, hc] = dot(low, tri[h, 0:nk, vc], ((1,), (0,))).astype(BF16)
            if backward:
                pbuf[rows, 0:nk] = low
                dp = dot(upb[rows, hc], tri[h, 0:nk, vc], ((1,), (1,)))
                inner = jnp.sum(p * dp, axis=-1, keepdims=True)
                ds = (p * (dp - inner) * scale).astype(BF16)
                dsbuf[rows, 0:nk] = ds
                cotb[h * 3, rows, :] = dot(ds, tri[h, 0:nk, kc], ((1,), (0,))).astype(BF16)

    teacher = m == 0

    def attend(h, *blocks):
        only(fake, (attention, h, blocks, True))
        only(teacher, (attention, h, blocks, False))

    def key_side(h, j):
        left, right = (
            (dsbuf, tri.at[h, :, pl.ds(0, 128)]) if j == 1 else (pbuf, upb.at[:, pl.ds(h * 128, 128)])
        )

        @pl.when(fake)
        def _():
            for b in range(4):
                first = max(0, (b - 1) * 128)
                rows = pl.ds(first, 512 - first)
                keys = pl.ds(b * 128, 128)
                cotb[h * 3 + j, keys, :] = dot(
                    left[rows, keys], right[rows, :], ((0,), (0,))
                ).astype(BF16)

    parts = (
        (0, 0, 2, False), (0, 2, 1, True),
        (1, 3, 1, False), (1, 4, 2, True),
        (2, 6, 2, False),
        (3, 8, 1, True),
    )
    groups = ((0, 3), (3, 3), (6, 2), (8, 1))

    def blocks_of(g):
        return range(groups[g][0], groups[g][0] + groups[g][1])

    def side_by_side(ref, g):
        return jnp.concatenate([ref[p] for p in blocks_of(g)], axis=1)

    def spread(g):
        for n, (pg, first, number, outer) in enumerate(parts):
            if pg == g:
                piece = cotb.at[pl.ds(first, number)]
                send(rcopy(piece, piece, cs.at[n], cr.at[n], out if outer else sib), fake)

    def direction_send():
        for dm in range(2):
            for dx in range(4):
                for dc in range(2):
                    tm, tx, tc = lax.rem(m + dm, 2), lax.rem(x + dx, nx), lax.rem(c + dc, 2)
                    src = attb.at[pl.ds(pl.multiple_of((tm * 8 + tx * 2 + tc) * 32, 32), 32), :]
                    dst = dbuf.at[m, x * 2 + yh]
                    sem = dr.at[dm, dx, yh]
                    cp = rcopy(src, dst, dsm, sem, at(m=tm, x=tx, c=tc, yh=c))
                    if dm + dx + dc == 0:
                        go(cp, away)

                        @pl.when(home)
                        def _():
                            pltpu.make_async_copy(src, dst, sem).start()
                    else:
                        go(cp)
        sent(attb.at[0:480, :], dsm, home)
        sent(attb, dsm, away)

    def exchange(g, cond):
        span = pl.ds(*groups[g])
        send(rcopy(cotb.at[span], coto.at[span], es.at[g], er.at[g], core_p), cond)

    def arrived(g):
        @pl.when(m == 0)
        def _():
            for n, (pg, first, number, _) in enumerate(parts):
                if pg == g:
                    wait_on(cotb.at[pl.ds(first, number)], cr.at[n])

    def partials(g):
        wait_on(coto.at[pl.ds(*groups[g])], er.at[g])
        mine, other = side_by_side(cotb, g), side_by_side(coto, g)
        for r in range(2):
            rows = pl.ds(r * 640, 640)
            both = dot(xts[c, rows, :], mine, ((1,), (0,))) + dot(xto[rows, :], other, ((1,), (0,)))
            for n, p in enumerate(blocks_of(g)):
                gbuf[p, rows, :] = both[:, n * 128 : (n + 1) * 128]

    def dest(o):
        return pl.multiple_of(lax.rem(z + nz + o, nz) * 160, 16)

    def span_of(d, k):
        return pl.ds(80 * d, 80) if k == 0 else pl.ds(0, 160)

    def ring(g, k):
        span = pl.ds(*groups[g])
        for d in range(2):
            o = (4 - k) if d == 0 else (k - 4)
            first = dest(o)
            mine, rest = pl.ds(80 * d, 80), pl.ds(80 - 80 * d, 80)
            if k >= 1:
                wait_on(rbuf.at[d, k - 1, span, span_of(d, k - 1), :], rr.at[d, g, k - 1])
            for p in blocks_of(g):
                if k == 0:
                    sbuf[d, k, p, mine, :] = gbuf[p, pl.ds(first + 80 * d, 80), :].astype(BF16)
                elif k == 1:
                    sbuf[d, k, p, mine, :] = (
                        gbuf[p, pl.ds(first + 80 * d, 80), :] + rbuf[d, 0, p, mine, :].astype(F32)
                    ).astype(BF16)
                    sbuf[d, k, p, rest, :] = gbuf[p, pl.ds(first + 80 - 80 * d, 80), :].astype(BF16)
                else:
                    sbuf[d, k, p, :, :] = (
                        gbuf[p, pl.ds(first, 160), :] + rbuf[d, k - 1, p, :, :].astype(F32)
                    ).astype(BF16)
            go(rcopy(
                sbuf.at[d, k, span, span_of(d, k), :], rbuf.at[d, k, span, span_of(d, k), :],
                rs.at[d, g, min(k, 1)], rr.at[d, g, k], up_z if d == 0 else dn_z,
            ))

    def ring_sent(g):
        span = pl.ds(*groups[g])
        for d in range(2):
            wait_on(sbuf.at[d, 0, span, span_of(d, 0), :], rs.at[d, g, 0])
            wait_on(sbuf.at[d, 1:4, span, :, :], rs.at[d, g, 1])

    def finish(g):
        for d in range(2):
            wait_on(rbuf.at[d, 3, pl.ds(*groups[g]), :, :], rr.at[d, g, 3])
        for p in blocks_of(g):
            fbuf[p] = (
                gbuf[p, pl.ds(dest(0), 160), :]
                + (rbuf[0, 3, p].astype(F32) + rbuf[1, 3, p].astype(F32))
            ).astype(BF16)

    def deliver(g):
        for n, (pg, first, number, outer) in enumerate(parts):
            if pg != g:
                continue
            piece = fbuf.at[pl.ds(first, number)]
            dst = obuf.at[pl.ds(first, number)]
            straight = (m == 1) if outer else (m <= 1)
            send(rcopy(piece, dst, fs.at[n, 0], fr.at[n], turn), jnp.logical_and(straight, away))

            @pl.when(jnp.logical_and(straight, home))
            def _():
                pltpu.make_async_copy(piece, dst, fr.at[n]).start()

            if outer:
                send(rcopy(piece, dst, fs.at[n, 1], fr.at[n], at(c=1 - yh, yh=c)), m == 0)

    def received(g):
        for n, (pg, first, number, _) in enumerate(parts):
            if pg == g:
                wait_on(obuf.at[pl.ds(first, number)], fr.at[n])
                for p in range(first, first + number):
                    grad_ref[p % 3, :, pl.ds(p // 3 * 128, 128)] = obuf[p]

    def direction():
        for dm in range(2):
            for dx in range(4):
                for b in range(2):
                    wait_on(dbuf.at[lax.rem(m + dm, 2), lax.rem(x + nx - dx, nx) * 2 + b], dr.at[dm, dx, b])
        for n in range(8):
            dir_ref[:, pl.ds(n * 384, 384)] = (dbuf[1, n].astype(F32) - dbuf[0, n].astype(F32)).astype(BF16)

    def shared(g):
        arrived(g)
        exchange(g, m == 0)

    def values_done(h):
        key_side(h, 2)
        if h == 2:
            spread(3)
            exchange(3, fake)

    def keys_done(h):
        key_side(h, 1)
        spread(h)
        exchange(h, fake)

    w_event(0, 0, 0, home)
    w_event(0, 0, 1, home)
    noise(0)
    x_own(0)
    noise(1)
    w_event(0, 0, 0, away)
    w_event(0, 0, 1, away)
    w_turn(1)
    stage(0, 1, 0)
    w_event(1, 0, 0, home)
    w_event(1, 0, 1, home)
    x_own(1)
    x_y(0)
    noise(2)
    stage(0, 1, 1)
    w_event(2, 0, 0, home)
    w_event(2, 0, 1, home)
    w_turn(2)
    x_own(2)
    x_y(1)
    stage(0, 2, 0)
    w_event(1, 0, 0, away)
    noise(3)
    x_own(3)
    x_z(0)
    stage(0, 2, 1)
    w_event(1, 0, 1, away)
    x_y(2)
    stage(0, 3, 0)
    x_z(1)
    stage(0, 3, 1)
    x_ready(0)
    turned(0)
    last(0)
    stage(1, 1, 0)
    x_y(3)
    x_z(2)
    stage(1, 1, 1)
    side_inputs()
    x_ready(1)
    turned(1)
    turned_send(0)
    stage(1, 2, 0)
    w_event(2, 0, 0, away)
    multiply_columns(0)
    multiply_columns(1)
    stage(1, 2, 1)
    w_event(2, 0, 1, away)
    x_z(3)
    x_ready(2)
    multiply_columns(2)
    turned(2)
    turned_send(1)
    stage(1, 3, 0)
    x_ready(3)
    multiply_columns(3)
    keep(0)
    stage(1, 3, 1)
    stage(2, 1, 0)
    attention_inputs()
    attend(0, 0, 1)
    multiply(1, 0, 1, 2)
    last(1)
    attend(0, 2, 3)
    values_done(0)
    keys_done(0)
    stage(2, 1, 1)
    multiply(1, 3, 4, 5, 6, 7)
    keep(1)
    stage(2, 2, 0)
    attend(1, 0, 1)
    stage(2, 2, 1)
    attend(1, 2, 3)
    values_done(1)
    keys_done(1)
    stage(2, 3, 0)
    turned(3)
    turned_send(2)
    turned_send(3)
    multiply(2, 0, 1, 2)
    stage(2, 3, 1)
    for q in range(2):
        wait_on(xto.at[pl.ds(q * 640, 640), :], xtr.at[q])
    shared(0)
    partials(0)
    ring(0, 0)
    multiply(2, 3, 4)
    only(fake, (partials, 1), (ring, 1, 0))
    early = len(pending)
    last(2)
    only(fake, (multiply, 2, 5, 6, 7), (keep, 2))
    ring(0, 1)
    shared(1)
    only(fake, (attention, 2, (0, 1), True), (ring, 1, 1), (attention, 2, (2, 3), True))
    values_done(2)
    keys_done(2)
    only(teacher, (partials, 1), (ring, 1, 0))
    ring(0, 2)
    only(teacher, (multiply, 2, 5, 6, 7), (keep, 2), (attention, 2, (0, 1), False), (ring, 1, 1))
    only(teacher, (attention, 2, (2, 3), False))
    only(fake, (ring, 1, 2))
    ring(0, 3)
    shared(3)
    only(teacher, (ring, 1, 2))
    shared(2)
    only(fake, (ring, 1, 3))
    partials(3)
    ring(3, 0)
    partials(2)
    ring(2, 0)
    only(teacher, (ring, 1, 3))
    direction_send()
    settle(early)
    finish(0)
    deliver(0)
    ring(3, 1)
    ring(2, 1)
    finish(1)
    deliver(1)
    ring(3, 2)
    ring(2, 2)
    direction()
    ring(3, 3)
    ring(2, 3)
    received(0)
    finish(3)
    deliver(3)
    finish(2)
    deliver(2)
    received(1)
    received(3)
    for g in range(4):
        ring_sent(g)
    received(2)
    settle(len(pending))


def widen_kernel(direction_ref, grads_ref, direction_out, grads_out):
    direction_out[...] = direction_ref[...]
    grads_out[...] = grads_ref[...].astype(F32)


def per_device(latents, noise, noise_level, group_index, projections, upstream):
    weights = jnp.transpose(projections[0], (1, 0, 2))
    groups = group_index
    dma = pltpu.SemaphoreType.DMA
    vmem = pltpu.VMEM
    anywhere = pl.BlockSpec(memory_space=pl.ANY)
    direction, grads = pl.pallas_call(
        step_kernel,
        out_shape=(
            jax.ShapeDtypeStruct((32, 3072), BF16),
            jax.ShapeDtypeStruct((3, 160, 384), BF16),
        ),
        in_specs=[anywhere, anywhere, pl.BlockSpec(memory_space=pltpu.SMEM), anywhere, anywhere, anywhere],
        out_specs=(pl.BlockSpec(memory_space=pltpu.VMEM), pl.BlockSpec(memory_space=pltpu.VMEM)),
        scratch_shapes=[
            vmem((3, 5120, 384), BF16),
            vmem((3, 2, 160, 384), BF16),
            vmem((4, 512, 1280), BF16),
            vmem((4, 256, 1280), BF16),
            vmem((4, 256, 1280), BF16),
            vmem((512, 384), F32),
            vmem((3, 512, 384), BF16),
            vmem((512, 384), BF16),
            vmem((1, 512), jnp.int32),
            vmem((512, 128), jnp.int32),
            vmem((512, 384), BF16),
            vmem((9, 512, 128), BF16),
            vmem((9, 512, 128), BF16),
            vmem((2, 1280, 512), BF16),
            vmem((1280, 512), BF16),
            vmem((512, 512), BF16),
            vmem((512, 512), BF16),
            vmem((9, 1280, 128), F32),
            vmem((2, 4, 9, 160, 128), BF16),
            vmem((2, 4, 9, 160, 128), BF16),
            vmem((9, 160, 128), BF16),
            vmem((9, 160, 128), BF16),
            vmem((2, 8, 32, 384), BF16),
            dma((3, 8, 2)), dma((3, 8)), dma((3,)), dma((3,)), dma((3,)), dma((3, 2)),
            dma((4, 2)), dma((4, 2)), dma((4,)), dma((4,)),
            dma((4, 2)), dma((4,)), dma((2,)), dma((2,)),
            dma((6,)), dma((6,)), dma((4,)), dma((4,)),
            dma((2, 4, 4)), dma((2, 4, 2)), dma((6,)), dma((6, 2)),
            dma((2, 4, 2)), dma,
        ],
        compiler_params=pltpu.CompilerParams(
            collective_id=0, has_side_effects=True, vmem_limit_bytes=62 << 20
        ),
    )(latents[0], noise[0], noise_level, weights, upstream[0], groups)
    direction, grads = pl.pallas_call(
        widen_kernel,
        out_shape=(
            jax.ShapeDtypeStruct((32, 3072), BF16),
            jax.ShapeDtypeStruct((3, 160, 384), F32),
        ),
        in_specs=[pl.BlockSpec(memory_space=pltpu.VMEM)] * 2,
        out_specs=(pl.BlockSpec(memory_space=pltpu.VMEM), pl.BlockSpec(memory_space=pltpu.VMEM)),
    )(direction, grads)
    return direction[None], jnp.transpose(grads, (1, 0, 2))


def solution(mesh):
    split = Mesh(
        mesh.devices.reshape(2, mesh.shape["seq"] // 2, 2, mesh.shape["fsdp"] // 2, 2), AXES
    )
    clip, heads = ("z", "yh"), ("x", "c")
    return jax.shard_map(
        per_device,
        mesh=split,
        in_specs=(
            P(clip, "m", None),
            P(clip, "m", None),
            P(clip),
            P(clip, None),
            P("m", clip, None, heads),
            P(clip, None, heads),
        ),
        out_specs=(P(clip, ("m", "x", "c"), None), P(("m", "z", "yh"), None, heads)),
        check_vma=False,
    )
```

```python
import math

import jax
import jax.numpy as jnp
from jax import lax
from jax.experimental import pallas as pl
from jax.experimental.pallas import tpu as pltpu
from jax.sharding import Mesh
from jax.sharding import PartitionSpec as P

HEAD = 128
AXES = ("m", "x", "c", "z", "yh")
MESH_ID = pl.DeviceIdType.MESH
F32 = jnp.float32
BF16 = jnp.bfloat16
OFFSETS = (0, -1, 1, -2, 2, -3, 3, 4)


def dot(a, b, dims):
    return lax.dot_general(a, b, (dims, ((), ())), preferred_element_type=F32)


def step_kernel(
    lat_ref, noi_ref, lvl_ref, proj_ref, up_ref, gi_ref,
    dir_ref, grad_ref,
    wbuf, own, xbuf, latv, noiv, acc, tri, upb, gib, gcol, attb, cotb, coto,
    xts, xto, pbuf, dsbuf, gbuf, sbuf, rbuf, fbuf, obuf, dbuf,
    wr, wc, ws, wcs, wos, wl, ya, xa, xs, xxs, lsem, usem, xtr, xtss, cr, cs, er, es,
    rr, rs, fr, fs, dr, dsm,
):
    m, x, c, z, yh = (lax.axis_index(a) for a in AXES)
    nz = lax.axis_size("z")
    nx = lax.axis_size("x")
    home = c == yh
    away = c != yh

    def at(**k):
        return k

    core_p = at(c=1 - c)
    sib = at(m=1 - m)
    out = at(m=1 - m, yh=1 - yh)
    turn = at(c=yh, yh=c)
    up_z = at(z=lax.rem(z + 1, nz))
    dn_z = at(z=lax.rem(z + nz - 1, nz))
    blk = [lax.rem(z + nz + o, nz) for o in OFFSETS]

    def rcopy(src, dst, ss, rsem, dev):
        return pltpu.make_async_remote_copy(
            src_ref=src, dst_ref=dst, send_sem=ss, recv_sem=rsem,
            device_id=dev, device_id_type=MESH_ID,
        )

    def wait_on(ref, sem):
        pltpu.make_async_copy(ref, ref, sem).wait()

    pending = []

    def go(cp, cond=None):
        if cond is None:
            cp.start()
        else:
            pl.when(cond)(cp.start)

    def send(cp, cond=None):
        go(cp, cond)
        pending.append((cp.wait_send, cond))

    def sent(ref, sem, cond=None):
        pending.append((lambda: wait_on(ref, sem), cond))

    def only(cond, *calls):
        @pl.when(cond)
        def _():
            for call, *arguments in calls:
                call(*arguments)

    def settle(number):
        for wait, cond in pending[:number]:
            if cond is None:
                wait()
            else:
                pl.when(cond)(wait)
        del pending[:number]

    rows_m = pl.ds(pl.multiple_of(m * 256, 256), 256)

    def read(p, which):
        src, dst = ((lat_ref, latv), (noi_ref, noiv))[which]
        return pltpu.make_async_copy(src.at[:, pl.ds(p * 1280, 1280)], dst.at[p], lsem.at[p, which])

    def w_rows(zb, core, i):
        return pl.ds(pl.multiple_of(zb * 640 + core * 320 + i * 160, 16), 160)

    def own_chunk(h, i):
        return wbuf.at[h, w_rows(z, yh, i), :]

    def stage_own(h, i, dst, sem):
        for j in range(3):
            pltpu.make_async_copy(
                proj_ref.at[j, pl.ds(160 * i, 160), pl.ds(128 * h, 128)],
                dst.at[:, pl.ds(128 * j, 128)], sem,
            ).start()

    @pl.when(home)
    def _():
        for h in range(3):
            for i in range(2):
                stage_own(h, i, own_chunk(h, i), wr.at[h, 0, i])
            if h < 2:
                for p in (2 * h, 2 * h + 1):
                    read(p, 0).start()
                    read(p, 1).start()

    @pl.when(away)
    def _():
        for h in range(3):
            for i in range(2):
                stage_own(h, i, own.at[h, i], wl.at[h, i])

    barrier = pltpu.get_barrier_semaphore()
    count = 0
    for dm in range(2):
        for dx in range(4):
            for dc in range(2):
                for dy in range(2):
                    if dm + dx + dc + dy == 0:
                        continue
                    peer = at(
                        m=lax.rem(m + dm, 2), x=lax.rem(x + dx, nx),
                        c=lax.rem(c + dc, 2), yh=lax.rem(yh + dy, 2),
                    )
                    pl.semaphore_signal(barrier, inc=1, device_id=peer, device_id_type=MESH_ID)
                    count += 1
    for peer in (up_z, dn_z):
        pl.semaphore_signal(barrier, inc=1, device_id=peer, device_id_type=MESH_ID)
        count += 1
    pl.semaphore_wait(barrier, count)

    def w_turn(h):
        for i in range(2):
            pl.when(away)(lambda: wait_on(own.at[h, i], wl.at[h, i]))
            go(rcopy(own.at[h, i], own_chunk(h, i), wos.at[h], wr.at[h, 0, i], turn), away)
        sent(wbuf.at[h, 0:320, :], wos.at[h], away)

    w_turn(0)

    def side_inputs():
        send(rcopy(gi_ref, gib, usem.at[2], usem.at[3], turn), away)
        send(rcopy(up_ref, upb, usem.at[0], usem.at[1], turn), jnp.logical_and(away, m == 1))

        @pl.when(jnp.logical_or(home, m == 0))
        def _():
            pltpu.make_async_copy(up_ref, upb, usem.at[1]).start()

        @pl.when(home)
        def _():
            pltpu.make_async_copy(gi_ref, gib, usem.at[3]).start()

    rate = lvl_ref[0]

    up_x = at(x=lax.rem(x + 1, nx))
    dn_x = at(x=lax.rem(x + nx - 1, nx))

    def quarter(half, step):
        first = half * 256 + lax.rem(x + nx + step, nx) * 64
        return pl.ds(pl.multiple_of(first, 64), 64)

    def noise(p):
        @pl.when(home)
        def _():
            read(p, 0).wait()
            read(p, 1).wait()
            for lo in (0, 640):
                xbuf[p, rows_m, lo : lo + 640] = (
                    (1.0 - rate) * latv[p, :, lo : lo + 640].astype(F32)
                    + rate * noiv[p, :, lo : lo + 640].astype(F32)
                ).astype(BF16)

    def x_own(p):
        for q in range(2):
            piece = xbuf.at[p, quarter(m, q), :]
            go(rcopy(piece, piece, xs.at[p], ya.at[p, 0], sib), home)
            go(rcopy(piece, piece, xs.at[p], ya.at[p, 0], out), home)

    def x_side(p, kind, q, cond):
        piece = xbuf.at[p, quarter((1 - m) if kind == 0 else m, q), :]
        go(rcopy(piece, piece, xxs.at[p], xa.at[p, kind], up_x if q == 0 else dn_x), cond)

    def x_y(p):
        wait_on(xbuf.at[p, 0:128, :], ya.at[p, 0])
        for q in range(2):
            piece = xbuf.at[p, quarter(1 - m, q), :]
            if p % 2 == 1:
                go(rcopy(piece, piece, xs.at[p], ya.at[p, 1], out), home)
            else:
                go(rcopy(piece, piece, xs.at[p], ya.at[p, 1], sib), away)
            x_side(p, 0, q, None)

    def x_z(p):
        @pl.when(away)
        def _():
            wait_on(xbuf.at[p, 0:128, :], ya.at[p, 1])

        for q in range(2):
            x_side(p, 1, q, away)

    def x_ready(p):
        wait_on(xbuf.at[p, 0:128, :], xa.at[p, 0])

        @pl.when(away)
        def _():
            wait_on(xbuf.at[p, 0:128, :], xa.at[p, 1])

        sent(xbuf.at[p, 0 : 256 + 128 * (p % 2), :], xs.at[p], home)
        if p % 2 == 0:
            sent(xbuf.at[p, 0:128, :], xs.at[p], away)
        sent(xbuf.at[p, 0:128, :], xxs.at[p], home)
        sent(xbuf.at[p, 0:256, :], xxs.at[p], away)

    def w_event(h, k, i, cond=None):
        piece = wbuf.at[h, w_rows(blk[k], c, i), :]
        if cond is None:
            wait_on(piece, wr.at[h, k, i])
        else:
            pl.when(cond)(lambda: wait_on(piece, wr.at[h, k, i]))
        o = OFFSETS[k]
        if -3 < o <= 0 or (o == -3 and i == 0):
            to = OFFSETS.index(o - 1 if o > -3 else 4)
            go(rcopy(piece, piece, ws.at[h], wr.at[h, to, i], up_z), cond)
        if 0 <= o < 3 or (o == 3 and i == 1):
            go(rcopy(piece, piece, ws.at[h], wr.at[h, OFFSETS.index(o + 1), i], dn_z), cond)
        go(rcopy(piece, piece, wcs.at[h], wc.at[h, k], core_p), cond)

    def stage(h, n, i):
        w_event(h, 2 * n - 1, i)
        w_event(h, 2 * n, i)

    def last(h):
        w_event(h, 7, 0)
        w_event(h, 7, 1)
        sent(wbuf.at[h, 0:2240, :], ws.at[h])
        sent(wbuf.at[h, 0:2560, :], wcs.at[h])

    def w_other(h, k):
        first = pl.multiple_of(blk[k] * 640 + (1 - c) * 320, 64)
        wait_on(wbuf.at[h, pl.ds(first, 320), :], wc.at[h, k])

    def gather(first, part):
        if first:
            acc[...] = part
        else:
            acc[...] += part

    def multiply_columns(p):
        if p == 0:
            for k in range(8):
                w_other(0, k)
        gather(p == 0, dot(xbuf[p], wbuf[0, p * 1280 : (p + 1) * 1280, :], ((1,), (0,))))

    def multiply(h, *blocks):
        for k in blocks:
            w_other(h, k)
            cols = pl.ds(pl.multiple_of(lax.rem(blk[k], 2) * 640, 128), 640)
            rows = pl.ds(pl.multiple_of(blk[k] * 640, 128), 640)
            gather(k == 0, dot(xbuf[blk[k] // 2, :, cols], wbuf[h, rows, :], ((1,), (0,))))

    def keep(h):
        tri[h] = acc[...].astype(BF16)

    def turned(p):
        @pl.when(m == p // 2)
        def _():
            base = (p % 2) * 640
            for i in range(10):
                t = xbuf[p, :, i * 128 : (i + 1) * 128].T
                r = i * 128
                while r < (i + 1) * 128:
                    end = min((i + 1) * 128, (r // 160 + 1) * 160)
                    first = base + (r // 320) * 160 + r % 160
                    xts[(r % 320) // 160, pl.ds(first, end - r), :] = t[r - i * 128 : end - i * 128, :]
                    r = end

    def turned_send(p):
        span = pl.ds((p % 2) * 640, 640)
        send(
            rcopy(xts.at[1 - c, span, :], xto.at[span, :], xtss.at[p % 2], xtr.at[p % 2], core_p),
            m == p // 2,
        )

    def attention_inputs():
        wait_on(gib, usem.at[3])
        wait_on(upb, usem.at[1])
        gcol[...] = jnp.transpose(jnp.broadcast_to(gib[...], (128, 512)))

    scale = 1.0 / math.sqrt(HEAD)
    fake = m == 1
    def attention(h, blocks, backward):
        qc, kc, vc = (pl.ds(j * 128, 128) for j in range(3))
        hc = pl.ds(h * 128, 128)
        for b in blocks:
            nk = min(512, (b + 2) * 128)
            rows = pl.ds(b * 128, 128)
            s = dot(tri[h, rows, qc], tri[h, 0:nk, kc], ((1,), (1,))) * scale
            mine = gcol[rows, :]
            visible = gib[0:1, 0:nk] <= jnp.concatenate([mine] * (nk // 128), axis=1)
            s = jnp.where(visible, s, F32(-1e30))
            w = jnp.exp(s - jnp.max(s, axis=-1, keepdims=True))
            p = w * (1.0 / jnp.sum(w, axis=-1, keepdims=True))
            low = p.astype(BF16)
            attb[rows, hc] = dot(low, tri[h, 0:nk, vc], ((1,), (0,))).astype(BF16)
            if backward:
                pbuf[rows, 0:nk] = low
                dp = dot(upb[rows, hc], tri[h, 0:nk, vc], ((1,), (1,)))
                inner = jnp.sum(p * dp, axis=-1, keepdims=True)
                ds = (p * (dp - inner) * scale).astype(BF16)
                dsbuf[rows, 0:nk] = ds
                cotb[h * 3, rows, :] = dot(ds, tri[h, 0:nk, kc], ((1,), (0,))).astype(BF16)

    teacher = m == 0

    def attend(h, *blocks):
        only(fake, (attention, h, blocks, True))
        only(teacher, (attention, h, blocks, False))

    def key_side(h, j):
        left, right = (
            (dsbuf, tri.at[h, :, pl.ds(0, 128)]) if j == 1 else (pbuf, upb.at[:, pl.ds(h * 128, 128)])
        )

        @pl.when(fake)
        def _():
            for b in range(4):
                first = max(0, (b - 1) * 128)
                rows = pl.ds(first, 512 - first)
                keys = pl.ds(b * 128, 128)
                cotb[h * 3 + j, keys, :] = dot(
                    left[rows, keys], right[rows, :], ((0,), (0,))
                ).astype(BF16)

    parts = (
        (0, 0, 2, False), (0, 2, 1, True),
        (1, 3, 1, False), (1, 4, 2, True),
        (2, 6, 2, False),
        (3, 8, 1, True),
    )
    groups = ((0, 3), (3, 3), (6, 2), (8, 1))

    def blocks_of(g):
        return range(groups[g][0], groups[g][0] + groups[g][1])

    def side_by_side(ref, g):
        return jnp.concatenate([ref[p] for p in blocks_of(g)], axis=1)

    def spread(g):
        for n, (pg, first, number, outer) in enumerate(parts):
            if pg == g:
                piece = cotb.at[pl.ds(first, number)]
                send(rcopy(piece, piece, cs.at[n], cr.at[n], out if outer else sib), fake)

    def direction_send():
        for dm in range(2):
            for dx in range(4):
                for dc in range(2):
                    tm, tx, tc = lax.rem(m + dm, 2), lax.rem(x + dx, nx), lax.rem(c + dc, 2)
                    src = attb.at[pl.ds(pl.multiple_of((tm * 8 + tx * 2 + tc) * 32, 32), 32), :]
                    dst = dbuf.at[m, x * 2 + yh]
                    sem = dr
                    cp = rcopy(src, dst, dsm, sem, at(m=tm, x=tx, c=tc, yh=c))
                    if dm + dx + dc == 0:
                        go(cp, away)

                        @pl.when(home)
                        def _():
                            pltpu.make_async_copy(src, dst, sem).start()
                    else:
                        go(cp)
        sent(attb.at[0:480, :], dsm, home)
        sent(attb, dsm, away)

    def exchange(g, cond):
        span = pl.ds(*groups[g])
        send(rcopy(cotb.at[span], coto.at[span], es.at[g], er.at[g], core_p), cond)

    def arrived(g):
        @pl.when(m == 0)
        def _():
            for n, (pg, first, number, _) in enumerate(parts):
                if pg == g:
                    wait_on(cotb.at[pl.ds(first, number)], cr.at[n])

    def partials(g):
        wait_on(coto.at[pl.ds(*groups[g])], er.at[g])
        mine, other = side_by_side(cotb, g), side_by_side(coto, g)
        for r in range(2):
            rows = pl.ds(r * 640, 640)
            both = dot(xts[c, rows, :], mine, ((1,), (0,))) + dot(xto[rows, :], other, ((1,), (0,)))
            for n, p in enumerate(blocks_of(g)):
                gbuf[p, rows, :] = both[:, n * 128 : (n + 1) * 128]

    def dest(o):
        return pl.multiple_of(lax.rem(z + nz + o, nz) * 160, 16)

    def span_of(d, k):
        return pl.ds(80 * d, 80) if k == 0 else pl.ds(0, 160)

    def ring(g, k):
        span = pl.ds(*groups[g])
        for d in range(2):
            o = (4 - k) if d == 0 else (k - 4)
            first = dest(o)
            mine, rest = pl.ds(80 * d, 80), pl.ds(80 - 80 * d, 80)
            if k >= 1:
                wait_on(rbuf.at[d, k - 1, span, span_of(d, k - 1), :], rr.at[d, g, k - 1])
            for p in blocks_of(g):
                if k == 0:
                    sbuf[d, k, p, mine, :] = gbuf[p, pl.ds(first + 80 * d, 80), :].astype(BF16)
                elif k == 1:
                    sbuf[d, k, p, mine, :] = (
                        gbuf[p, pl.ds(first + 80 * d, 80), :] + rbuf[d, 0, p, mine, :].astype(F32)
                    ).astype(BF16)
                    sbuf[d, k, p, rest, :] = gbuf[p, pl.ds(first + 80 - 80 * d, 80), :].astype(BF16)
                else:
                    sbuf[d, k, p, :, :] = (
                        gbuf[p, pl.ds(first, 160), :] + rbuf[d, k - 1, p, :, :].astype(F32)
                    ).astype(BF16)
            go(rcopy(
                sbuf.at[d, k, span, span_of(d, k), :], rbuf.at[d, k, span, span_of(d, k), :],
                rs.at[g, min(k, 1)], rr.at[d, g, k], up_z if d == 0 else dn_z,
            ))

    def ring_sent(g):
        span = pl.ds(*groups[g])
        wait_on(sbuf.at[0, 0, span, :, :], rs.at[g, 0])
        wait_on(sbuf.at[:, 1:4, span, :, :], rs.at[g, 1])

    def finish(g):
        for d in range(2):
            wait_on(rbuf.at[d, 3, pl.ds(*groups[g]), :, :], rr.at[d, g, 3])
        for p in blocks_of(g):
            fbuf[p] = (
                gbuf[p, pl.ds(dest(0), 160), :]
                + (rbuf[0, 3, p].astype(F32) + rbuf[1, 3, p].astype(F32))
            ).astype(BF16)

    def deliver(g):
        for n, (pg, first, number, outer) in enumerate(parts):
            if pg != g:
                continue
            piece = fbuf.at[pl.ds(first, number)]
            dst = obuf.at[pl.ds(first, number)]
            straight = (m == 1) if outer else (m <= 1)
            send(rcopy(piece, dst, fs.at[n, 0], fr.at[n], turn), jnp.logical_and(straight, away))

            @pl.when(jnp.logical_and(straight, home))
            def _():
                pltpu.make_async_copy(piece, dst, fr.at[n]).start()

            if outer:
                send(rcopy(piece, dst, fs.at[n, 1], fr.at[n], at(c=1 - yh, yh=c)), m == 0)

    def received(g):
        for n, (pg, first, number, _) in enumerate(parts):
            if pg == g:
                wait_on(obuf.at[pl.ds(first, number)], fr.at[n])
                for p in range(first, first + number):
                    grad_ref[p % 3, :, pl.ds(p // 3 * 128, 128)] = obuf[p]

    def direction():
        wait_on(dbuf, dr)
        for n in range(8):
            dir_ref[:, pl.ds(n * 384, 384)] = (dbuf[1, n].astype(F32) - dbuf[0, n].astype(F32)).astype(BF16)

    def shared(g):
        arrived(g)
        exchange(g, m == 0)

    def values_done(h):
        key_side(h, 2)
        if h == 2:
            spread(3)
            exchange(3, fake)

    def keys_done(h):
        key_side(h, 1)
        spread(h)
        exchange(h, fake)

    w_event(0, 0, 0, home)
    w_event(0, 0, 1, home)
    noise(0)
    x_own(0)
    noise(1)
    w_event(0, 0, 0, away)
    w_event(0, 0, 1, away)
    w_turn(1)
    stage(0, 1, 0)
    w_event(1, 0, 0, home)
    w_event(1, 0, 1, home)
    x_own(1)
    x_y(0)
    noise(2)
    stage(0, 1, 1)
    w_event(2, 0, 0, home)
    w_event(2, 0, 1, home)
    w_turn(2)
    x_own(2)
    x_y(1)
    stage(0, 2, 0)
    w_event(1, 0, 0, away)
    noise(3)
    x_own(3)
    x_z(0)
    stage(0, 2, 1)
    w_event(1, 0, 1, away)
    x_y(2)
    stage(0, 3, 0)
    x_z(1)
    stage(0, 3, 1)
    x_ready(0)
    turned(0)
    last(0)
    stage(1, 1, 0)
    x_y(3)
    x_z(2)
    stage(1, 1, 1)
    side_inputs()
    x_ready(1)
    turned(1)
    turned_send(0)
    stage(1, 2, 0)
    w_event(2, 0, 0, away)
    multiply_columns(0)
    multiply_columns(1)
    stage(1, 2, 1)
    w_event(2, 0, 1, away)
    x_z(3)
    x_ready(2)
    multiply_columns(2)
    turned(2)
    turned_send(1)
    stage(1, 3, 0)
    x_ready(3)
    multiply_columns(3)
    keep(0)
    stage(1, 3, 1)
    stage(2, 1, 0)
    attention_inputs()
    attend(0, 0, 1)
    multiply(1, 0, 1, 2)
    last(1)
    attend(0, 2, 3)
    values_done(0)
    keys_done(0)
    stage(2, 1, 1)
    multiply(1, 3, 4, 5, 6, 7)
    keep(1)
    stage(2, 2, 0)
    attend(1, 0, 1)
    stage(2, 2, 1)
    attend(1, 2, 3)
    values_done(1)
    keys_done(1)
    stage(2, 3, 0)
    turned(3)
    turned_send(2)
    turned_send(3)
    multiply(2, 0, 1, 2)
    stage(2, 3, 1)
    for q in range(2):
        wait_on(xto.at[pl.ds(q * 640, 640), :], xtr.at[q])
    shared(0)
    partials(0)
    ring(0, 0)
    multiply(2, 3, 4)
    only(fake, (partials, 1), (ring, 1, 0))
    early = len(pending)
    last(2)
    only(fake, (multiply, 2, 5, 6, 7), (keep, 2))
    ring(0, 1)
    shared(1)
    only(fake, (attention, 2, (0, 1), True), (ring, 1, 1), (attention, 2, (2, 3), True))
    values_done(2)
    keys_done(2)
    only(teacher, (partials, 1), (ring, 1, 0))
    ring(0, 2)
    only(teacher, (multiply, 2, 5, 6, 7), (keep, 2), (attention, 2, (0, 1), False), (ring, 1, 1))
    only(teacher, (attention, 2, (2, 3), False))
    only(fake, (ring, 1, 2))
    ring(0, 3)
    shared(3)
    only(teacher, (ring, 1, 2))
    shared(2)
    only(fake, (ring, 1, 3))
    partials(3)
    ring(3, 0)
    partials(2)
    ring(2, 0)
    only(teacher, (ring, 1, 3))
    direction_send()
    settle(early)
    finish(0)
    deliver(0)
    ring(3, 1)
    ring(2, 1)
    finish(1)
    deliver(1)
    ring(3, 2)
    ring(2, 2)
    direction()
    ring(3, 3)
    ring(2, 3)
    received(0)
    finish(3)
    deliver(3)
    finish(2)
    deliver(2)
    received(1)
    received(3)
    for g in range(4):
        ring_sent(g)
    received(2)
    settle(len(pending))


def widen_kernel(direction_ref, grads_ref, direction_out, grads_out):
    direction_out[...] = direction_ref[...]
    grads_out[...] = grads_ref[...].astype(F32)


def per_device(latents, noise, noise_level, group_index, projections, upstream):
    weights = jnp.transpose(projections[0], (1, 0, 2))
    groups = group_index
    dma = pltpu.SemaphoreType.DMA
    vmem = pltpu.VMEM
    anywhere = pl.BlockSpec(memory_space=pl.ANY)
    direction, grads = pl.pallas_call(
        step_kernel,
        out_shape=(
            jax.ShapeDtypeStruct((32, 3072), BF16),
            jax.ShapeDtypeStruct((3, 160, 384), BF16),
        ),
        in_specs=[anywhere, anywhere, pl.BlockSpec(memory_space=pltpu.SMEM), anywhere, anywhere, anywhere],
        out_specs=(pl.BlockSpec(memory_space=pltpu.VMEM), pl.BlockSpec(memory_space=pltpu.VMEM)),
        scratch_shapes=[
            vmem((3, 5120, 384), BF16),
            vmem((3, 2, 160, 384), BF16),
            vmem((4, 512, 1280), BF16),
            vmem((4, 256, 1280), BF16),
            vmem((4, 256, 1280), BF16),
            vmem((512, 384), F32),
            vmem((3, 512, 384), BF16),
            vmem((512, 384), BF16),
            vmem((1, 512), jnp.int32),
            vmem((512, 128), jnp.int32),
            vmem((512, 384), BF16),
            vmem((9, 512, 128), BF16),
            vmem((9, 512, 128), BF16),
            vmem((2, 1280, 512), BF16),
            vmem((1280, 512), BF16),
            vmem((512, 512), BF16),
            vmem((512, 512), BF16),
            vmem((9, 1280, 128), F32),
            vmem((2, 4, 9, 160, 128), BF16),
            vmem((2, 4, 9, 160, 128), BF16),
            vmem((9, 160, 128), BF16),
            vmem((9, 160, 128), BF16),
            vmem((2, 8, 32, 384), BF16),
            dma((3, 8, 2)), dma((3, 8)), dma((3,)), dma((3,)), dma((3,)), dma((3, 2)),
            dma((4, 2)), dma((4, 2)), dma((4,)), dma((4,)),
            dma((4, 2)), dma((4,)), dma((2,)), dma((2,)),
            dma((6,)), dma((6,)), dma((4,)), dma((4,)),
            dma((2, 4, 4)), dma((4, 2)), dma((6,)), dma((6, 2)),
            dma, dma,
        ],
        compiler_params=pltpu.CompilerParams(
            collective_id=0, has_side_effects=True, vmem_limit_bytes=62 << 20
        ),
    )(latents[0], noise[0], noise_level, weights, upstream[0], groups)
    direction, grads = pl.pallas_call(
        widen_kernel,
        out_shape=(
            jax.ShapeDtypeStruct((32, 3072), BF16),
            jax.ShapeDtypeStruct((3, 160, 384), F32),
        ),
        in_specs=[pl.BlockSpec(memory_space=pltpu.VMEM)] * 2,
        out_specs=(pl.BlockSpec(memory_space=pltpu.VMEM), pl.BlockSpec(memory_space=pltpu.VMEM)),
    )(direction, grads)
    return direction[None], jnp.transpose(grads, (1, 0, 2))


def solution(mesh):
    split = Mesh(
        mesh.devices.reshape(2, mesh.shape["seq"] // 2, 2, mesh.shape["fsdp"] // 2, 2), AXES
    )
    clip, heads = ("z", "yh"), ("x", "c")
    return jax.shard_map(
        per_device,
        mesh=split,
        in_specs=(
            P(clip, "m", None),
            P(clip, "m", None),
            P(clip),
            P(clip, None),
            P("m", clip, None, heads),
            P(clip, None, heads),
        ),
        out_specs=(P(clip, ("m", "x", "c"), None), P(("m", "z", "yh"), None, heads)),
        check_vma=False,
    )
```
